32 devices in a mesh: guide: 2 (over core), blk: 16 (over z, y, x).
Axes of the slice: x: 2, y: 2, z: 4, core: 2. Of those that a mesh axis runs over, the one named last changes fastest.
Arguments:
- x_cols: bfloat16 [128, 2048], P(None, 'blk'), may hold values from -3 to 3
- queries: bfloat16 [128, 9216], P('blk'), may hold values from -64 to 64
- new_kv: bfloat16 [128, 576], P('blk'), may hold values from -6 to 6
- cache: bfloat16 [2, 128, 256, 576], P('guide', 'blk'), may hold values from -8 to 8
- lengths: int32 [2, 128], P('guide'), may hold values from 2 to 256, as said below
- perm: int32 [128], replicated, may hold values from 0 to 127, each once
- guide_scale: float32 [128], replicated, may hold values from 1.5 to 7.5
- w_uv: bfloat16 [16, 512, 128], replicated, may hold values from -0.75 to 0.75
- w_out: bfloat16 [2048, 2048], P(None, 'blk'), may hold values from -0.125 to 0.125
- mlp_gain: float32 [2048], replicated, may hold values from 0.5 to 1.5
- w_gate: bfloat16 [2048, 10944], P(None, 'blk'), may hold values from -0.125 to 0.125
- w_up: bfloat16 [2048, 10944], P(None, 'blk'), may hold values from -0.125 to 0.125
- w_down: bfloat16 [10944, 2048], P('blk'), may hold values from -0.0546875 to 0.0546875
- head_gain: float32 [2048], replicated, may hold values from 0.5 to 1.5
- w_head: bfloat16 [2048, 102400], P(None, 'blk'), may hold values from -0.125 to 0.125
Outputs:
- guided: bfloat16 [128, 102400], P('guide', 'blk')
The draws below stay inside these ranges and needn't reach their ends.
Inputs may be any that keep to these rules, and one draw needn't show every extreme that they name: Positions 0 to lengths[g, r] - 1 of request r's cache in group g are live; each group has a request with 256 live positions. Slot s holds request perm[s]; every request has one slot.
All inputs are finite; a program needn't handle non-finite values.
Results may differ from the reference program's by a relative error of at most 0.018.
Values may be sent and summed in bfloat16 or wider, within the bound.
No kernel may reach another device: no remote copies, remote signals or barrier semaphores. Data moves between devices by JAX's collectives and lax.ppermute only.
A program may use at most 128 MiB of HBM per device.

```python
import jax
import jax.numpy as jnp
from jax import lax

D = 2048
HEADS = 16
NOPE = 128
ROPE = 64
LATENT = 512
FF = 10944
VOCAB = 102400
MAXLEN = 256
REQUESTS = 128
FF_PAD = 10944


def draw_cache(key, part):
    full = jax.random.normal(jax.random.fold_in(key, 37), (2, REQUESTS, MAXLEN, LATENT + ROPE), jnp.float32)
    full = jnp.clip(full, -6.0, 6.0)
    return full.astype(jnp.bfloat16)


def draw_queries(key, part):
    drawn = jax.random.normal(jax.random.fold_in(key, 21), (REQUESTS, HEADS, LATENT + ROPE), jnp.float32)
    drawn = jnp.clip(drawn, -6.0, 6.0)
    return drawn.reshape(REQUESTS, HEADS * (LATENT + ROPE)).astype(jnp.bfloat16)


def draw_lengths(key, part):
    counts = jax.random.randint(jax.random.fold_in(key, 43), (2, REQUESTS), 2, MAXLEN + 1)
    picked = jax.random.randint(jax.random.fold_in(key, 47), (2, 1), 0, REQUESTS)
    positions = jnp.arange(REQUESTS, dtype=jnp.int32)[None, :]
    return jnp.where(positions == picked, MAXLEN, counts).astype(jnp.int32)


def level_of(own_key, shape, split, smallest, top_value):
    loudness = 1.0
    for axis_at, shards_of in split:
        heights = jax.random.uniform(jax.random.fold_in(jax.random.fold_in(own_key, 6), axis_at), (shards_of,), jnp.float32, smallest / len(split), top_value / len(split))
        loudness = loudness * jnp.repeat(jnp.exp(heights), shape[axis_at] // shards_of).reshape((-1,) + (1,) * (len(shape) - 1 - axis_at))
    return loudness


def gaussian(key, dims, deviation, most, pieces=(), kind=jnp.bfloat16):
    values = deviation * jax.random.normal(key, dims, jnp.float32)
    if pieces:
        values = values * level_of(key, dims, pieces, -0.22, 0.18)
    return jnp.clip(values, -most, most).astype(kind)


def setup_inputs(seed: int = 0) -> dict:
    splits = jax.random.split(jax.random.key(seed), 16)
    return {
        "x_cols": gaussian(splits[0], (REQUESTS, D), 0.5, 3.0, ((1, 16),)),
        "queries": draw_queries(jax.random.fold_in(splits[15], 71), 0),
        "new_kv": gaussian(splits[2], (REQUESTS, LATENT + ROPE), 1.0, 6.0, ((0, 16),)),
        "cache": draw_cache(jax.random.fold_in(splits[15], 71), 0),
        "lengths": draw_lengths(jax.random.fold_in(splits[15], 71), 0),
        "perm": jax.random.permutation(splits[5], REQUESTS).astype(jnp.int32),
        "guide_scale": jnp.clip(jax.random.uniform(splits[6], (REQUESTS,), jnp.float32, 1.5, 7.5), 1.5, 7.5),
        "w_uv": gaussian(splits[7], (HEADS, LATENT, NOPE), 64 ** -0.5, 0.75),
        "w_out": gaussian(splits[8], (HEADS * NOPE, D), (HEADS * NOPE) ** -0.5, 0.125, ((1, 16),)),
        "mlp_gain": jnp.clip(1.0 + 0.1 * jax.random.normal(splits[9], (D,), jnp.float32), 0.5, 1.5),
        "w_gate": gaussian(splits[10], (D, FF_PAD), D ** -0.5, 0.125, ((1, 16),)),
        "w_up": gaussian(splits[11], (D, FF_PAD), D ** -0.5, 0.125, ((1, 16),)),
        "w_down": gaussian(splits[12], (FF_PAD, D), FF ** -0.5, 0.0546875, ((0, 16),)),
        "head_gain": jnp.clip(1.0 + 0.1 * jax.random.normal(splits[13], (D,), jnp.float32), 0.5, 1.5),
        "w_head": gaussian(splits[14], (D, VOCAB), D ** -0.5, 0.125, ((1, 16),)),
    }


def rms_round(hidden, gain):
    values = hidden.astype(jnp.float32)
    meansq = lax.optimization_barrier(jnp.mean(values * values, axis=-1, keepdims=True))
    return (values * lax.rsqrt(meansq + 1e-06) * gain).astype(jnp.bfloat16)

def attend_one(query_heads, new_key, cached_keys, live_len):
    score_scale = (NOPE + ROPE) ** (-0.5)
    query_f = query_heads.astype(jnp.float32)
    keys_f = cached_keys.astype(jnp.float32)
    new_f = new_key.astype(jnp.float32)
    scores = jnp.einsum('hk,lk->hl', query_f, keys_f) * score_scale
    own_score = jnp.einsum('hk,k->h', query_f, new_f) * score_scale
    live_mask = jnp.arange(MAXLEN, dtype=jnp.int32)[None, :] < live_len
    scores = jnp.where(live_mask, scores, jnp.float32(-1e+30))
    peak_score = jnp.maximum(lax.optimization_barrier(jnp.max(scores, axis=-1)), own_score)
    probs = jnp.where(live_mask, jnp.exp(scores - peak_score[:, None]), jnp.float32(0.0))
    own_prob = jnp.exp(own_score - peak_score)
    softmax_total = lax.optimization_barrier(jnp.sum(probs, axis=-1)) + own_prob
    weights = (probs / softmax_total[:, None]).astype(jnp.bfloat16)
    own_weight = (own_prob / softmax_total).astype(jnp.bfloat16)
    latent_out = jnp.einsum('hl,lc->hc', weights.astype(jnp.float32), keys_f[:, :LATENT])
    latent_out = latent_out + own_weight.astype(jnp.float32)[:, None] * new_f[None, :LATENT]
    return latent_out.astype(jnp.bfloat16)

def reference(x_cols, queries, new_kv, cache, lengths, perm, guide_scale, w_uv, w_out, mlp_gain, w_gate, w_up, w_down, head_gain, w_head):
    query_all = queries.reshape(REQUESTS, HEADS, LATENT + ROPE)

    def branch_logits(group_id):
        live_len = lengths[group_id][perm].astype(jnp.int32)
        latent_out = lax.map(lambda items: attend_one(*items), (query_all, new_kv, cache[group_id], live_len))
        value_rows = jnp.einsum('rhc,hcd->rhd', latent_out.astype(jnp.float32), w_uv.astype(jnp.float32))
        value_rows = value_rows.astype(jnp.bfloat16).reshape(REQUESTS, HEADS * NOPE)
        residual = (x_cols.astype(jnp.float32) + jnp.dot(value_rows, w_out, preferred_element_type=jnp.float32)).astype(jnp.bfloat16)
        normed = rms_round(residual, mlp_gain)
        gate_out = jnp.dot(normed, w_gate[:, :FF], preferred_element_type=jnp.float32)
        up_out = jnp.dot(normed, w_up[:, :FF], preferred_element_type=jnp.float32)
        hidden = (jax.nn.silu(gate_out) * up_out).astype(jnp.bfloat16)
        after_mlp = (residual.astype(jnp.float32) + jnp.dot(hidden, w_down[:FF], preferred_element_type=jnp.float32)).astype(jnp.bfloat16)
        return jnp.dot(rms_round(after_mlp, head_gain), w_head, preferred_element_type=jnp.float32)
    cond_logits = branch_logits(0)
    uncond_logits = branch_logits(1)
    slot_scale = guide_scale[perm]
    mixed = (uncond_logits + slot_scale[:, None] * (cond_logits - uncond_logits)).astype(jnp.bfloat16)
    request_order = jnp.zeros((REQUESTS,), jnp.int32).at[perm].set(jnp.arange(REQUESTS, dtype=jnp.int32))
    return mixed[request_order]
```

```python
import jax
import jax.numpy as jnp
from jax import lax
from jax.experimental import pallas as pl
from jax.experimental.pallas import tpu as pltpu
from jax.sharding import PartitionSpec as P

FF = 10944
BF = jnp.bfloat16
F32 = jnp.float32
NN = (((1,), (0,)), ((), ()))
NT = (((1,), (1,)), ((), ()))
TN = (((0,), (0,)), ((), ()))
VM = pl.BlockSpec(memory_space=pltpu.VMEM)
SM = pl.BlockSpec(memory_space=pltpu.SMEM)
HB = pl.BlockSpec(memory_space=pltpu.HBM)


def partner(value, axis, apart):
    mask = 2**apart
    pairs = [(source, source ^ mask) for source in range(lax.axis_size(axis))]
    return lax.ppermute(value, axis, pairs)


def swap(value, mask):
    pairs = [(source, source ^ mask) for source in range(lax.axis_size("blk"))]
    return lax.ppermute(value, "blk", pairs)


def rms_round(hidden, gain):
    values = hidden.astype(jnp.float32)
    meansq = jnp.mean(values * values, axis=-1, keepdims=True)
    return (values * lax.rsqrt(meansq + 1e-06) * gain).astype(jnp.bfloat16)


def cost(micros):
    return pl.CostEstimate(flops=int(micros * 1e9), bytes_accessed=int(micros * 3e6), transcendentals=0)


def iota(shape, dim):
    return lax.broadcasted_iota(jnp.int32, shape, dim)


def dot(a, b, dims, precision=None):
    return lax.dot_general(a, b, dims, precision=precision, preferred_element_type=F32)


def attend_kernel(
    ids, perm_h, lengths_h, queries_h, new_h, cache, w_uv, out,
    perm, lengths, queries, new_kv, qs, keys, up, sems, others,
):
    slots, width, positions = cache.shape
    heads, latent, nope = w_uv.shape
    rows = heads * slots
    first = ids[1] * slots
    small = [
        pltpu.make_async_copy(source, target, others.at[k])
        for k, (source, target) in enumerate(
            ((queries_h, queries), (new_h, new_kv), (perm_h, perm), (lengths_h, lengths))
        )
    ]
    copies = [
        pltpu.make_async_copy(cache.at[s], keys.at[s], sems.at[s]) for s in range(slots)
    ]
    upcopy = pltpu.make_async_copy(w_uv, up, others.at[4])
    for copy in small + copies + [upcopy]:
        copy.start()
    small[0].wait()
    for h in range(heads):
        qs[h * slots : (h + 1) * slots, :] = queries[:, h * width : (h + 1) * width]
    q = qs[...]
    small[1].wait()
    new = new_kv[...]
    scale = (nope + width - latent) ** (-0.5)
    slot_of = iota((rows, 1), 0) % slots
    own = dot(q, new, NT)
    own = jnp.sum(jnp.where(iota((rows, slots), 1) == slot_of, own, 0.0), 1, keepdims=True) * scale
    small[2].wait()
    small[3].wait()
    live = jnp.zeros((rows, 1), jnp.int32)
    for s in range(slots):
        live = jnp.where(slot_of == s, lengths[0, perm[first + s]], live)
    scores = jnp.zeros((rows, positions), F32)
    for s in range(slots):
        copies[s].wait()
        scores = jnp.where(slot_of == s, dot(q, keys[s], NN), scores)
    mask = iota((rows, positions), 1) < live
    scores = jnp.where(mask, scores * scale, -1e30)
    peak = jnp.maximum(jnp.max(scores, axis=1, keepdims=True), own)
    probs = jnp.where(mask, jnp.exp(scores - peak), 0.0)
    own = jnp.exp(own - peak)
    total = jnp.sum(probs, axis=1, keepdims=True) + own
    weights = probs / total
    own = (own / total).astype(BF).astype(F32)
    mixed = jnp.zeros((rows, latent), F32)
    for s in range(slots):
        part = jnp.where(slot_of == s, weights, 0.0).astype(BF)
        mixed += dot(part, keys[s, :latent, :], NT)
    mixed += own * jnp.tile(new[:, :latent].astype(F32), (heads, 1))
    upcopy.wait()
    for h in range(heads):
        rows_h = mixed[h * slots : (h + 1) * slots, :].astype(BF)
        out[:, h * nope : (h + 1) * nope] = dot(rows_h, up[h], NN).astype(BF)


def attend(ids, perm, lengths, queries, new_kv, cache, w_uv):
    slots, width, positions = cache.shape
    heads, latent, nope = w_uv.shape
    return pl.pallas_call(
        attend_kernel,
        out_shape=jax.ShapeDtypeStruct((slots, heads * nope), BF),
        in_specs=[SM] + [HB] * 6,
        out_specs=VM,
        scratch_shapes=[
            pltpu.SMEM(perm.shape, jnp.int32),
            pltpu.SMEM(lengths.shape, jnp.int32),
            pltpu.VMEM(queries.shape, BF),
            pltpu.VMEM(new_kv.shape, BF),
            pltpu.VMEM((heads * slots, width), BF),
            pltpu.VMEM((slots, width, positions), BF),
            pltpu.VMEM((heads, latent, nope), BF),
            pltpu.SemaphoreType.DMA((slots,)),
            pltpu.SemaphoreType.DMA((5,)),
        ],
        compiler_params=pltpu.CompilerParams(vmem_limit_bytes=60 << 20),
        cost_estimate=cost(15),
        name="attend",
    )(ids, perm, lengths, queries, new_kv, cache, w_uv)


def request_of(row, rows):
    chip = ((row >> 3) & 3) * 4 + (row >> 5)
    return ((row >> 2) & 1) * (rows // 2) + chip * 4 + (row & 3)


def project_kernel(ids, perm, v0, v1, v2, v3, w_out, x_cols, out):
    blk = ids[1]
    rows = x_cols.shape[0]
    w = w_out[...]
    attended = jnp.concatenate([dot(v[...], w, NN) for v in (v0, v1, v2, v3)], axis=0)
    shape = (rows, rows)
    wanted = request_of(iota(shape, 0), rows)
    by_slot = (jnp.broadcast_to(perm[...], shape) == wanted).astype(F32)
    arrived = iota(shape, 1)
    slot = ((blk ^ (((arrived >> 3) & 3) * 4) ^ (arrived >> 5)) << 3) | (arrived & 7)
    move = (iota(shape, 0) == slot).astype(F32)
    by_arrival = dot(by_slot.astype(BF), move.astype(BF), NN)
    moved = dot(by_arrival, attended, NN, lax.Precision.HIGHEST)
    base = dot(by_slot.astype(BF), x_cols[...], NN)
    out[...] = (base + moved).astype(BF)


def project(ids, perm, pieces, w_out, x_cols):
    return pl.pallas_call(
        project_kernel,
        out_shape=jax.ShapeDtypeStruct(x_cols.shape, BF),
        in_specs=[SM] + [VM] * 7,
        out_specs=VM,
        compiler_params=pltpu.CompilerParams(vmem_limit_bytes=4 << 20),
        cost_estimate=cost(15),
        name="project",
    )(ids, perm, *pieces, w_out, x_cols)


def feed_kernel(
    ids, r0, r1, r2, r3, gain, w_gate, w_up, w_down, own, c1, c2, c3, kept, full, acc
):
    blk = ids[1]
    groups, rows, cols = r0.shape
    units = w_gate.shape[0]
    for q, ref in enumerate((r0, r1, r2, r3)):
        for j in range(groups):
            at = pl.multiple_of((blk ^ (4 * j) ^ q) * cols, cols)
            full[:, pl.ds(at, cols)] = ref[j].astype(F32)
    values = full[...]
    meansq = jnp.mean(values * values, axis=1, keepdims=True)
    normed = (values * lax.rsqrt(meansq + 1e-06) * gain[...]).astype(BF)
    gate = dot(normed, w_gate[...], NT)
    up = dot(normed, w_up[...], NT)
    unit = blk * units + iota((rows, units), 1)
    hidden = gate * (1.0 / (1.0 + jnp.exp(-gate))) * up
    hidden = jnp.where(unit < FF, hidden, 0.0).astype(BF)
    acc[...] = dot(hidden, w_down[...], NN)
    low, high = blk & 3, blk >> 2
    chunk = rows // 4
    for q, ref in enumerate((own, c1, c2, c3)):
        at = pl.multiple_of((low ^ q) * chunk, chunk)
        ref[...] = acc[pl.ds(at, chunk), :].astype(ref.dtype)
    small = chunk // 4
    at = pl.multiple_of(low * chunk + high * small, small)
    kept[...] = full[pl.ds(at, small), :]


def feed(ids, pieces, gain, w_gate, w_up, w_down):
    groups, rows, cols = pieces[0].shape
    width = w_down.shape[1]
    part = (rows // 4, width)
    return pl.pallas_call(
        feed_kernel,
        out_shape=[
            jax.ShapeDtypeStruct(part, F32),
            jax.ShapeDtypeStruct(part, BF),
            jax.ShapeDtypeStruct(part, BF),
            jax.ShapeDtypeStruct(part, BF),
            jax.ShapeDtypeStruct((rows // 16, width), F32),
        ],
        in_specs=[SM] + [VM] * 8,
        out_specs=[VM] * 5,
        scratch_shapes=[pltpu.VMEM((rows, width), F32), pltpu.VMEM((rows, width), F32)],
        compiler_params=pltpu.CompilerParams(vmem_limit_bytes=8 << 20),
        cost_estimate=cost(15),
        name="feed",
    )(ids, *pieces, gain, w_gate, w_up, w_down)


def reduce_kernel(ids, own, p1, p2, p3, keep, o1, o2, o3, acc):
    high = ids[1] >> 2
    acc[...] = own[...] + p1[...].astype(F32) + p2[...].astype(F32) + p3[...].astype(F32)
    small = keep.shape[0]
    for j, ref in enumerate((keep, o1, o2, o3)):
        at = pl.multiple_of((high ^ j) * small, small)
        ref[...] = acc[pl.ds(at, small), :].astype(ref.dtype)


def reduce_part(ids, own, parts):
    rows, width = own.shape
    small = (rows // 4, width)
    return pl.pallas_call(
        reduce_kernel,
        out_shape=[jax.ShapeDtypeStruct(small, F32)] + [jax.ShapeDtypeStruct(small, BF)] * 3,
        in_specs=[SM] + [VM] * 4,
        out_specs=[VM] * 4,
        scratch_shapes=[pltpu.VMEM((rows, width), F32)],
        compiler_params=pltpu.CompilerParams(vmem_limit_bytes=2 << 20),
        cost_estimate=cost(20),
        name="reduce_part",
    )(ids, own, *parts)


def finish_kernel(ids, own, p1, p2, p3, kept, gain, stay, go):
    total = own[...] + p1[...].astype(F32) + p2[...].astype(F32) + p3[...].astype(F32)
    after = (kept[...] + total).astype(BF).astype(F32)
    meansq = jnp.mean(after * after, axis=1, keepdims=True)
    normed = after * lax.rsqrt(meansq + 1e-06) * gain[...]
    half = normed.shape[0] // 2
    first, last = normed[:half], normed[half:]
    lower = ids[0] == 0
    stay[...] = jnp.where(lower, first, last).astype(BF)
    go[...] = jnp.where(lower, last, first).astype(BF)


def finish(ids, own, parts, kept, gain):
    rows, width = own.shape
    return pl.pallas_call(
        finish_kernel,
        out_shape=[jax.ShapeDtypeStruct((rows // 2, width), BF)] * 2,
        in_specs=[SM] + [VM] * 6,
        out_specs=[VM] * 2,
        compiler_params=pltpu.CompilerParams(vmem_limit_bytes=1 << 20),
        cost_estimate=cost(20),
        name="finish",
    )(ids, own, *parts, kept, gain)


def head_kernel(ids, r0, r1, r2, r3, scale, w_head, out, full, factor):
    guide, blk = ids[0], ids[1]
    part = r0.shape[0]
    rows = 4 * part
    half = rows // 2

    @pl.when(pl.program_id(0) == 0)
    def _():
        wanted = iota((rows, part), 0)
        total = None
        for q, ref in enumerate((r0, r1, r2, r3)):
            at = iota((rows, part), 1)
            chip = blk ^ ((at >> 3) << 2) ^ q
            row = (((at >> 2) & 1) ^ guide) * half + chip * 4 + (at & 3)
            piece = dot((row == wanted).astype(BF), ref[...], NN)
            total = piece if total is None else total + piece
        full[...] = total.astype(BF)
        mine = iota((half, rows), 0) + guide * half == iota((half, rows), 1)
        factor[...] = jnp.sum(
            jnp.where(mine, jnp.broadcast_to(scale[...], (half, rows)), 0.0), 1, keepdims=True
        )

    logits = dot(full[...], w_head[...], NN)
    cond, uncond = logits[:half], logits[half:]
    out[...] = (uncond + factor[...] * (cond - uncond)).astype(BF)


def head(ids, pieces, scale, w_head):
    part, width = pieces[0].shape
    rows = 4 * part
    vocab = w_head.shape[1]
    tile = next(t for t in (640, 512, 256, 128, vocab) if vocab % t == 0)
    whole = pl.BlockSpec((part, width), lambda i: (0, 0))
    return pl.pallas_call(
        head_kernel,
        out_shape=jax.ShapeDtypeStruct((rows // 2, vocab), BF),
        grid=(vocab // tile,),
        in_specs=[SM]
        + [whole] * 4
        + [
            pl.BlockSpec((1, rows), lambda i: (0, 0)),
            pl.BlockSpec((width, tile), lambda i: (0, i)),
        ],
        out_specs=pl.BlockSpec((rows // 2, tile), lambda i: (0, i)),
        scratch_shapes=[pltpu.VMEM((rows, width), BF), pltpu.VMEM((rows // 2, 1), F32)],
        compiler_params=pltpu.CompilerParams(vmem_limit_bytes=48 << 20),
        cost_estimate=cost(8),
        name="head",
    )(ids, *pieces, scale, w_head)


def spread(value):
    near = [value] + [swap(value, mask) for mask in (4, 8, 12)]
    group = jnp.concatenate(near, axis=0)
    return [group] + [swap(group, mask) for mask in (1, 2, 3)]


def fast_body(
    x_cols,
    queries,
    new_kv,
    cache,
    lengths,
    perm,
    guide_scale,
    w_uv,
    w_out,
    mlp_gain,
    w_gate,
    w_up,
    w_down,
    head_gain,
    w_head,
):
    guide_index = lax.axis_index("guide")
    blk_index = lax.axis_index("blk")
    ids = jnp.stack([guide_index, blk_index]).astype(jnp.int32)
    rows, cols = x_cols.shape
    keys = jnp.swapaxes(cache[0], 1, 2)
    values = attend(ids, perm, lengths, queries, new_kv, keys, w_uv)
    residual = project(ids, perm[None], spread(values), w_out, x_cols)
    pieces = [piece.reshape(4, rows, cols) for piece in spread(residual)]
    own, *chunks, kept = feed(
        ids, pieces, mlp_gain[None], jnp.swapaxes(w_gate, 0, 1), jnp.swapaxes(w_up, 0, 1), w_down
    )
    arrived = [swap(chunk, mask) for chunk, mask in zip(chunks, (1, 2, 3))]
    own, *chunks = reduce_part(ids, own, arrived)
    arrived = [swap(chunk, mask) for chunk, mask in zip(chunks, (4, 8, 12))]
    stay, go = finish(ids, own, arrived, kept, head_gain[None])
    normed = jnp.concatenate([stay, partner(go, "guide", 0)], axis=0)
    return head(ids, spread(normed), guide_scale[None], w_head)


def body(
    x_cols,
    queries,
    new_kv,
    cache,
    lengths,
    perm,
    guide_scale,
    w_uv,
    w_out,
    mlp_gain,
    w_gate,
    w_up,
    w_down,
    head_gain,
    w_head,
):
    guide_index = lax.axis_index("guide")
    blk_index = lax.axis_index("blk")
    slots_dev = queries.shape[0]
    heads_count = w_uv.shape[0]
    latent_size = w_uv.shape[1]
    key_width = new_kv.shape[1]
    score_scale = (w_uv.shape[2] + key_width - latent_size) ** (-0.5)
    slot_ids = blk_index * slots_dev + jnp.arange(slots_dev, dtype=jnp.int32)
    owners = jnp.take(perm, slot_ids)
    live_len = jnp.take(lengths[0], owners)
    query_heads = queries.reshape(slots_dev, heads_count, key_width)
    cached_keys = cache[0]
    scores = (
        jnp.einsum("shk,slk->shl", query_heads, cached_keys, preferred_element_type=jnp.float32)
        * score_scale
    )
    own_score = (
        jnp.einsum("shk,sk->sh", query_heads, new_kv, preferred_element_type=jnp.float32)
        * score_scale
    )
    live_mask = (
        jnp.arange(cached_keys.shape[1], dtype=jnp.int32)[None, None, :] < live_len[:, None, None]
    )
    scores = jnp.where(live_mask, scores, jnp.float32(-1e30))
    peak_score = jnp.maximum(jnp.max(scores, axis=-1), own_score)
    probs = jnp.where(live_mask, jnp.exp(scores - peak_score[..., None]), jnp.float32(0.0))
    own_prob = jnp.exp(own_score - peak_score)
    softmax_total = jnp.sum(probs, axis=-1) + own_prob
    weights = (probs / softmax_total[..., None]).astype(jnp.bfloat16)
    own_weight = (own_prob / softmax_total).astype(jnp.bfloat16)
    latent_out = jnp.einsum(
        "shl,slc->shc", weights, cached_keys[:, :, :latent_size], preferred_element_type=jnp.float32
    )
    latent_out = latent_out + own_weight.astype(jnp.float32)[..., None] * new_kv[
        :, None, :latent_size
    ].astype(jnp.float32)
    value_rows = jnp.einsum(
        "shc,hcd->shd", latent_out.astype(jnp.bfloat16), w_uv, preferred_element_type=jnp.float32
    )
    value_rows = value_rows.astype(jnp.bfloat16).reshape(slots_dev, -1)
    attended = jnp.dot(
        lax.all_gather(value_rows, "blk", axis=0, tiled=True),
        w_out,
        preferred_element_type=jnp.float32,
    )
    residual = (x_cols.astype(jnp.float32) + attended).astype(jnp.bfloat16)
    rows_full = lax.all_gather(residual, "blk", axis=1, tiled=True)
    normed = rms_round(rows_full, mlp_gain)
    unit_count = w_gate.shape[1]
    gate_out = jnp.dot(normed, w_gate, preferred_element_type=jnp.float32)
    up_out = jnp.dot(normed, w_up, preferred_element_type=jnp.float32)
    unit_ids = blk_index * unit_count + jnp.arange(unit_count, dtype=jnp.int32)
    hidden = jnp.where(
        unit_ids[None, :] < FF, jax.nn.silu(gate_out) * up_out, jnp.float32(0.0)
    ).astype(jnp.bfloat16)
    partial_sum = jnp.dot(hidden, w_down, preferred_element_type=jnp.float32)
    summed = lax.psum(partial_sum, "blk")
    after_mlp = (rows_full.astype(jnp.float32) + summed).astype(jnp.bfloat16)
    logits = jnp.dot(rms_round(after_mlp, head_gain), w_head, preferred_element_type=jnp.float32)
    request_count = logits.shape[0]
    half_rows = request_count // 2
    slot_scale = jnp.take(guide_scale, perm)
    request_order = (
        jnp.zeros((request_count,), jnp.int32)
        .at[perm]
        .set(jnp.arange(request_count, dtype=jnp.int32))
    )
    own_order = lax.dynamic_slice_in_dim(request_order, guide_index * half_rows, half_rows)
    other_logits = partner(logits.astype(jnp.bfloat16), "guide", 0).astype(logits.dtype)
    cond_logits = jnp.where(guide_index == 0, logits, other_logits)
    uncond_logits = jnp.where(guide_index == 0, other_logits, logits)
    mixed = (uncond_logits + slot_scale[:, None] * (cond_logits - uncond_logits)).astype(
        jnp.bfloat16
    )
    return jnp.take(mixed, own_order, axis=0)


def solution(mesh):
    def run(*args):
        chips = mesh.shape["blk"]
        rows, width = args[0].shape
        fits = chips == 16 and rows == 128 and mesh.shape["guide"] == 2 and width % (128 * chips) == 0
        return jax.shard_map(
            fast_body if fits else body,
            mesh=mesh,
            in_specs=(
                P(None, "blk"),
                P("blk", None),
                P("blk", None),
                P("guide", "blk", None, None),
                P("guide", None),
                P(),
                P(),
                P(),
                P(None, "blk"),
                P(),
                P(None, "blk"),
                P(None, "blk"),
                P("blk", None),
                P(),
                P(None, "blk"),
            ),
            out_specs=P("guide", "blk"),
            check_vma=False,
        )(*args)

    return run
```

```python
import jax
import jax.numpy as jnp
from jax import lax
from jax.experimental import pallas as pl
from jax.experimental.pallas import tpu as pltpu
from jax.sharding import PartitionSpec as P

FF = 10944
BF = jnp.bfloat16
F32 = jnp.float32
NN = (((1,), (0,)), ((), ()))
NT = (((1,), (1,)), ((), ()))
TN = (((0,), (0,)), ((), ()))
VM = pl.BlockSpec(memory_space=pltpu.VMEM)
SM = pl.BlockSpec(memory_space=pltpu.SMEM)
HB = pl.BlockSpec(memory_space=pltpu.HBM)


def partner(value, axis, apart):
    mask = 2**apart
    pairs = [(source, source ^ mask) for source in range(lax.axis_size(axis))]
    return lax.ppermute(value, axis, pairs)


def swap(value, mask):
    pairs = [(source, source ^ mask) for source in range(lax.axis_size("blk"))]
    return lax.ppermute(value, "blk", pairs)


def rms_round(hidden, gain):
    values = hidden.astype(jnp.float32)
    meansq = jnp.mean(values * values, axis=-1, keepdims=True)
    return (values * lax.rsqrt(meansq + 1e-06) * gain).astype(jnp.bfloat16)


def cost(micros):
    return pl.CostEstimate(flops=int(micros * 1e9), bytes_accessed=int(micros * 3e6), transcendentals=0)


def iota(shape, dim):
    return lax.broadcasted_iota(jnp.int32, shape, dim)


def dot(a, b, dims, precision=None):
    return lax.dot_general(a, b, dims, precision=precision, preferred_element_type=F32)


def attend_kernel(
    ids, perm_h, lengths_h, queries_h, new_h, cache, w_uv, out,
    perm, lengths, queries, new_kv, qs, keys, up, sems, others,
):
    slots, width, positions = cache.shape
    heads, latent, nope = w_uv.shape
    rows = heads * slots
    first = ids[1] * slots
    small = [
        pltpu.make_async_copy(source, target, others.at[k])
        for k, (source, target) in enumerate(
            ((queries_h, queries), (new_h, new_kv), (perm_h, perm), (lengths_h, lengths))
        )
    ]
    copies = [
        pltpu.make_async_copy(cache.at[s], keys.at[s], sems.at[s]) for s in range(slots)
    ]
    upcopy = pltpu.make_async_copy(w_uv, up, others.at[4])
    for copy in small + copies + [upcopy]:
        copy.start()
    small[0].wait()
    for h in range(heads):
        qs[h * slots : (h + 1) * slots, :] = queries[:, h * width : (h + 1) * width]
    q = qs[...]
    small[1].wait()
    new = new_kv[...]
    scale = (nope + width - latent) ** (-0.5)
    slot_of = iota((rows, 1), 0) % slots
    own = dot(q, new, NT)
    own = jnp.sum(jnp.where(iota((rows, slots), 1) == slot_of, own, 0.0), 1, keepdims=True) * scale
    small[2].wait()
    small[3].wait()
    live = jnp.zeros((rows, 1), jnp.int32)
    for s in range(slots):
        live = jnp.where(slot_of == s, lengths[0, perm[first + s]], live)
    scores = jnp.zeros((rows, positions), F32)
    for s in range(slots):
        copies[s].wait()
        scores = jnp.where(slot_of == s, dot(q, keys[s], NN), scores)
    mask = iota((rows, positions), 1) < live
    scores = jnp.where(mask, scores * scale, -1e30)
    peak = jnp.maximum(jnp.max(scores, axis=1, keepdims=True), own)
    probs = jnp.where(mask, jnp.exp(scores - peak), 0.0)
    own = jnp.exp(own - peak)
    total = jnp.sum(probs, axis=1, keepdims=True) + own
    weights = probs / total
    own = (own / total).astype(BF).astype(F32)
    mixed = jnp.zeros((rows, latent), F32)
    for s in range(slots):
        part = jnp.where(slot_of == s, weights, 0.0).astype(BF)
        mixed += dot(part, keys[s, :latent, :], NT)
    mixed += own * jnp.tile(new[:, :latent].astype(F32), (heads, 1))
    upcopy.wait()
    for h in range(heads):
        rows_h = mixed[h * slots : (h + 1) * slots, :].astype(BF)
        out[:, h * nope : (h + 1) * nope] = dot(rows_h, up[h], NN).astype(BF)


def attend(ids, perm, lengths, queries, new_kv, cache, w_uv):
    slots, width, positions = cache.shape
    heads, latent, nope = w_uv.shape
    return pl.pallas_call(
        attend_kernel,
        out_shape=jax.ShapeDtypeStruct((slots, heads * nope), BF),
        in_specs=[SM] + [HB] * 6,
        out_specs=VM,
        scratch_shapes=[
            pltpu.SMEM(perm.shape, jnp.int32),
            pltpu.SMEM(lengths.shape, jnp.int32),
            pltpu.VMEM(queries.shape, BF),
            pltpu.VMEM(new_kv.shape, BF),
            pltpu.VMEM((heads * slots, width), BF),
            pltpu.VMEM((slots, width, positions), BF),
            pltpu.VMEM((heads, latent, nope), BF),
            pltpu.SemaphoreType.DMA((slots,)),
            pltpu.SemaphoreType.DMA((5,)),
        ],
        compiler_params=pltpu.CompilerParams(vmem_limit_bytes=60 << 20),
        cost_estimate=cost(15),
        name="attend",
    )(ids, perm, lengths, queries, new_kv, cache, w_uv)


def request_of(row, rows):
    chip = ((row >> 3) & 3) * 4 + (row >> 5)
    return ((row >> 2) & 1) * (rows // 2) + chip * 4 + (row & 3)


def project_kernel(ids, perm, v0, v1, v2, v3, w_out, x_cols, out):
    blk = ids[1]
    rows = x_cols.shape[0]
    w = w_out[...]
    attended = jnp.concatenate([dot(v[...], w, NN) for v in (v0, v1, v2, v3)], axis=0)
    shape = (rows, rows)
    wanted = request_of(iota(shape, 0), rows)
    by_slot = (jnp.broadcast_to(perm[...], shape) == wanted).astype(F32)
    arrived = iota(shape, 1)
    slot = ((blk ^ (((arrived >> 3) & 3) * 4) ^ (arrived >> 5)) << 3) | (arrived & 7)
    move = (iota(shape, 0) == slot).astype(F32)
    by_arrival = dot(by_slot.astype(BF), move.astype(BF), NN)
    moved = dot(by_arrival, attended, NN, lax.Precision.HIGHEST)
    base = dot(by_slot.astype(BF), x_cols[...], NN)
    out[...] = (base + moved).astype(BF)


def project(ids, perm, pieces, w_out, x_cols):
    return pl.pallas_call(
        project_kernel,
        out_shape=jax.ShapeDtypeStruct(x_cols.shape, BF),
        in_specs=[SM] + [VM] * 7,
        out_specs=VM,
        compiler_params=pltpu.CompilerParams(vmem_limit_bytes=4 << 20),
        cost_estimate=cost(15),
        name="project",
    )(ids, perm, *pieces, w_out, x_cols)


def feed_kernel(
    ids, r0, r1, r2, r3, gain, w_gate, w_up, w_down, own, c1, c2, c3, kept, full, acc
):
    blk = ids[1]
    groups, rows, cols = r0.shape
    units = w_gate.shape[0]
    for q, ref in enumerate((r0, r1, r2, r3)):
        for j in range(groups):
            at = pl.multiple_of((blk ^ (4 * j) ^ q) * cols, cols)
            full[:, pl.ds(at, cols)] = ref[j].astype(F32)
    values = full[...]
    meansq = jnp.mean(values * values, axis=1, keepdims=True)
    normed = (values * lax.rsqrt(meansq + 1e-06) * gain[...]).astype(BF)
    gate = dot(normed, w_gate[...], NT)
    up = dot(normed, w_up[...], NT)
    unit = blk * units + iota((rows, units), 1)
    hidden = gate * (1.0 / (1.0 + jnp.exp(-gate))) * up
    hidden = jnp.where(unit < FF, hidden, 0.0).astype(BF)
    acc[...] = dot(hidden, w_down[...], NN)
    low, high = blk & 3, blk >> 2
    chunk = rows // 4
    for q, ref in enumerate((own, c1, c2, c3)):
        at = pl.multiple_of((low ^ q) * chunk, chunk)
        ref[...] = acc[pl.ds(at, chunk), :].astype(ref.dtype)
    small = chunk // 4
    at = pl.multiple_of(low * chunk + high * small, small)
    kept[...] = full[pl.ds(at, small), :]


def feed(ids, pieces, gain, w_gate, w_up, w_down):
    groups, rows, cols = pieces[0].shape
    width = w_down.shape[1]
    part = (rows // 4, width)
    return pl.pallas_call(
        feed_kernel,
        out_shape=[
            jax.ShapeDtypeStruct(part, F32),
            jax.ShapeDtypeStruct(part, BF),
            jax.ShapeDtypeStruct(part, BF),
            jax.ShapeDtypeStruct(part, BF),
            jax.ShapeDtypeStruct((rows // 16, width), F32),
        ],
        in_specs=[SM] + [VM] * 8,
        out_specs=[VM] * 5,
        scratch_shapes=[pltpu.VMEM((rows, width), F32), pltpu.VMEM((rows, width), F32)],
        compiler_params=pltpu.CompilerParams(vmem_limit_bytes=8 << 20),
        cost_estimate=cost(15),
        name="feed",
    )(ids, *pieces, gain, w_gate, w_up, w_down)


def reduce_kernel(ids, own, p1, p2, p3, keep, o1, o2, o3, acc):
    high = ids[1] >> 2
    acc[...] = own[...] + p1[...].astype(F32) + p2[...].astype(F32) + p3[...].astype(F32)
    small = keep.shape[0]
    for j, ref in enumerate((keep, o1, o2, o3)):
        at = pl.multiple_of((high ^ j) * small, small)
        ref[...] = acc[pl.ds(at, small), :].astype(ref.dtype)


def reduce_part(ids, own, parts):
    rows, width = own.shape
    small = (rows // 4, width)
    return pl.pallas_call(
        reduce_kernel,
        out_shape=[jax.ShapeDtypeStruct(small, F32)] + [jax.ShapeDtypeStruct(small, BF)] * 3,
        in_specs=[SM] + [VM] * 4,
        out_specs=[VM] * 4,
        scratch_shapes=[pltpu.VMEM((rows, width), F32)],
        compiler_params=pltpu.CompilerParams(vmem_limit_bytes=2 << 20),
        cost_estimate=cost(20),
        name="reduce_part",
    )(ids, own, *parts)


def finish_kernel(ids, own, p1, p2, p3, kept, gain, stay, go):
    total = own[...] + p1[...].astype(F32) + p2[...].astype(F32) + p3[...].astype(F32)
    after = (kept[...] + total).astype(BF).astype(F32)
    meansq = jnp.mean(after * after, axis=1, keepdims=True)
    normed = after * lax.rsqrt(meansq + 1e-06) * gain[...]
    half = normed.shape[0] // 2
    first, last = normed[:half], normed[half:]
    lower = ids[0] == 0
    stay[...] = jnp.where(lower, first, last).astype(BF)
    go[...] = jnp.where(lower, last, first).astype(BF)


def finish(ids, own, parts, kept, gain):
    rows, width = own.shape
    return pl.pallas_call(
        finish_kernel,
        out_shape=[jax.ShapeDtypeStruct((rows // 2, width), BF)] * 2,
        in_specs=[SM] + [VM] * 6,
        out_specs=[VM] * 2,
        compiler_params=pltpu.CompilerParams(vmem_limit_bytes=1 << 20),
        cost_estimate=cost(20),
        name="finish",
    )(ids, own, *parts, kept, gain)


def head_kernel(ids, r0, r1, r2, r3, scale, w_head, out, full, factor):
    guide, blk = ids[0], ids[1]
    part = r0.shape[0]
    rows = 4 * part
    half = rows // 2
    vocab = w_head.shape[1]
    tile = next(t for t in (1280, 256, 128) if vocab % t == 0)
    wanted = iota((rows, part), 0)
    total = None
    for q, ref in enumerate((r0, r1, r2, r3)):
        at = iota((rows, part), 1)
        chip = blk ^ ((at >> 3) << 2) ^ q
        row = (((at >> 2) & 1) ^ guide) * half + chip * 4 + (at & 3)
        piece = dot((row == wanted).astype(BF), ref[...], NN)
        total = piece if total is None else total + piece
    full[...] = total.astype(BF)
    mine = iota((half, rows), 0) + guide * half == iota((half, rows), 1)
    factor[...] = jnp.sum(
        jnp.where(mine, jnp.broadcast_to(scale[...], (half, rows)), 0.0), 1, keepdims=True
    )

    @pl.loop(0, vocab // tile)
    def _(step):
        at = pl.ds(pl.multiple_of(step * tile, tile), tile)
        logits = dot(full[...], w_head[:, at], NN)
        cond, uncond = logits[:half], logits[half:]
        out[:, at] = (uncond + factor[...] * (cond - uncond)).astype(BF)


def head(ids, pieces, scale, w_head):
    part, width = pieces[0].shape
    rows = 4 * part
    vocab = w_head.shape[1]
    return pl.pallas_call(
        head_kernel,
        out_shape=jax.ShapeDtypeStruct((rows // 2, vocab), BF),
        in_specs=[SM] + [VM] * 6,
        out_specs=VM,
        scratch_shapes=[pltpu.VMEM((rows, width), BF), pltpu.VMEM((rows // 2, 1), F32)],
        compiler_params=pltpu.CompilerParams(vmem_limit_bytes=8 << 20),
        cost_estimate=cost(8),
        name="head",
    )(ids, *pieces, scale, w_head)


def join_kernel(*refs):
    out = refs[-1]
    part = refs[0].shape[0]
    for k, ref in enumerate(refs[:-1]):
        out[k * part : (k + 1) * part, :] = ref[...]


def join(parts):
    rows, width = parts[0].shape
    return pl.pallas_call(
        join_kernel,
        out_shape=jax.ShapeDtypeStruct((len(parts) * rows, width), parts[0].dtype),
        in_specs=[VM] * len(parts),
        out_specs=VM,
        compiler_params=pltpu.CompilerParams(vmem_limit_bytes=1 << 20),
        cost_estimate=cost(1),
        name="join",
    )(*parts)


def spread(value):
    group = join([value] + [swap(value, mask) for mask in (4, 8, 12)])
    return [group] + [swap(group, mask) for mask in (1, 2, 3)]


def fast_body(
    x_cols,
    queries,
    new_kv,
    cache,
    lengths,
    perm,
    guide_scale,
    w_uv,
    w_out,
    mlp_gain,
    w_gate,
    w_up,
    w_down,
    head_gain,
    w_head,
):
    guide_index = lax.axis_index("guide")
    blk_index = lax.axis_index("blk")
    ids = jnp.stack([guide_index, blk_index]).astype(jnp.int32)
    rows, cols = x_cols.shape
    keys = jnp.swapaxes(cache[0], 1, 2)
    values = attend(ids, perm, lengths, queries, new_kv, keys, w_uv)
    residual = project(ids, perm[None], spread(values), w_out, x_cols)
    pieces = [piece.reshape(4, rows, cols) for piece in spread(residual)]
    own, *chunks, kept = feed(
        ids, pieces, mlp_gain[None], jnp.swapaxes(w_gate, 0, 1), jnp.swapaxes(w_up, 0, 1), w_down
    )
    arrived = [swap(chunk, mask) for chunk, mask in zip(chunks, (1, 2, 3))]
    own, *chunks = reduce_part(ids, own, arrived)
    arrived = [swap(chunk, mask) for chunk, mask in zip(chunks, (4, 8, 12))]
    stay, go = finish(ids, own, arrived, kept, head_gain[None])
    normed = join([stay, partner(go, "guide", 0)])
    return head(ids, spread(normed), guide_scale[None], w_head)


def body(
    x_cols,
    queries,
    new_kv,
    cache,
    lengths,
    perm,
    guide_scale,
    w_uv,
    w_out,
    mlp_gain,
    w_gate,
    w_up,
    w_down,
    head_gain,
    w_head,
):
    guide_index = lax.axis_index("guide")
    blk_index = lax.axis_index("blk")
    slots_dev = queries.shape[0]
    heads_count = w_uv.shape[0]
    latent_size = w_uv.shape[1]
    key_width = new_kv.shape[1]
    score_scale = (w_uv.shape[2] + key_width - latent_size) ** (-0.5)
    slot_ids = blk_index * slots_dev + jnp.arange(slots_dev, dtype=jnp.int32)
    owners = jnp.take(perm, slot_ids)
    live_len = jnp.take(lengths[0], owners)
    query_heads = queries.reshape(slots_dev, heads_count, key_width)
    cached_keys = cache[0]
    scores = (
        jnp.einsum("shk,slk->shl", query_heads, cached_keys, preferred_element_type=jnp.float32)
        * score_scale
    )
    own_score = (
        jnp.einsum("shk,sk->sh", query_heads, new_kv, preferred_element_type=jnp.float32)
        * score_scale
    )
    live_mask = (
        jnp.arange(cached_keys.shape[1], dtype=jnp.int32)[None, None, :] < live_len[:, None, None]
    )
    scores = jnp.where(live_mask, scores, jnp.float32(-1e30))
    peak_score = jnp.maximum(jnp.max(scores, axis=-1), own_score)
    probs = jnp.where(live_mask, jnp.exp(scores - peak_score[..., None]), jnp.float32(0.0))
    own_prob = jnp.exp(own_score - peak_score)
    softmax_total = jnp.sum(probs, axis=-1) + own_prob
    weights = (probs / softmax_total[..., None]).astype(jnp.bfloat16)
    own_weight = (own_prob / softmax_total).astype(jnp.bfloat16)
    latent_out = jnp.einsum(
        "shl,slc->shc", weights, cached_keys[:, :, :latent_size], preferred_element_type=jnp.float32
    )
    latent_out = latent_out + own_weight.astype(jnp.float32)[..., None] * new_kv[
        :, None, :latent_size
    ].astype(jnp.float32)
    value_rows = jnp.einsum(
        "shc,hcd->shd", latent_out.astype(jnp.bfloat16), w_uv, preferred_element_type=jnp.float32
    )
    value_rows = value_rows.astype(jnp.bfloat16).reshape(slots_dev, -1)
    attended = jnp.dot(
        lax.all_gather(value_rows, "blk", axis=0, tiled=True),
        w_out,
        preferred_element_type=jnp.float32,
    )
    residual = (x_cols.astype(jnp.float32) + attended).astype(jnp.bfloat16)
    rows_full = lax.all_gather(residual, "blk", axis=1, tiled=True)
    normed = rms_round(rows_full, mlp_gain)
    unit_count = w_gate.shape[1]
    gate_out = jnp.dot(normed, w_gate, preferred_element_type=jnp.float32)
    up_out = jnp.dot(normed, w_up, preferred_element_type=jnp.float32)
    unit_ids = blk_index * unit_count + jnp.arange(unit_count, dtype=jnp.int32)
    hidden = jnp.where(
        unit_ids[None, :] < FF, jax.nn.silu(gate_out) * up_out, jnp.float32(0.0)
    ).astype(jnp.bfloat16)
    partial_sum = jnp.dot(hidden, w_down, preferred_element_type=jnp.float32)
    summed = lax.psum(partial_sum, "blk")
    after_mlp = (rows_full.astype(jnp.float32) + summed).astype(jnp.bfloat16)
    logits = jnp.dot(rms_round(after_mlp, head_gain), w_head, preferred_element_type=jnp.float32)
    request_count = logits.shape[0]
    half_rows = request_count // 2
    slot_scale = jnp.take(guide_scale, perm)
    request_order = (
        jnp.zeros((request_count,), jnp.int32)
        .at[perm]
        .set(jnp.arange(request_count, dtype=jnp.int32))
    )
    own_order = lax.dynamic_slice_in_dim(request_order, guide_index * half_rows, half_rows)
    other_logits = partner(logits.astype(jnp.bfloat16), "guide", 0).astype(logits.dtype)
    cond_logits = jnp.where(guide_index == 0, logits, other_logits)
    uncond_logits = jnp.where(guide_index == 0, other_logits, logits)
    mixed = (uncond_logits + slot_scale[:, None] * (cond_logits - uncond_logits)).astype(
        jnp.bfloat16
    )
    return jnp.take(mixed, own_order, axis=0)


def solution(mesh):
    def run(*args):
        chips = mesh.shape["blk"]
        rows, width = args[0].shape
        fits = chips == 16 and rows == 128 and mesh.shape["guide"] == 2 and width % (128 * chips) == 0
        return jax.shard_map(
            fast_body if fits else body,
            mesh=mesh,
            in_specs=(
                P(None, "blk"),
                P("blk", None),
                P("blk", None),
                P("guide", "blk", None, None),
                P("guide", None),
                P(),
                P(),
                P(),
                P(None, "blk"),
                P(),
                P(None, "blk"),
                P(None, "blk"),
                P("blk", None),
                P(),
                P(None, "blk"),
            ),
            out_specs=P("guide", "blk"),
            check_vma=False,
        )(*args)

    return run
```

```python
import jax
import jax.numpy as jnp
from jax import lax
from jax.experimental import pallas as pl
from jax.experimental.pallas import tpu as pltpu
from jax.sharding import PartitionSpec as P

FF = 10944
BF = jnp.bfloat16
F32 = jnp.float32
NN = (((1,), (0,)), ((), ()))
NT = (((1,), (1,)), ((), ()))
TN = (((0,), (0,)), ((), ()))
VM = pl.BlockSpec(memory_space=pltpu.VMEM)
HB = pl.BlockSpec(memory_space=pltpu.HBM)


def partner(value, axis, apart):
    mask = 2**apart
    pairs = [(source, source ^ mask) for source in range(lax.axis_size(axis))]
    return lax.ppermute(value, axis, pairs)


def swap(value, mask):
    pairs = [(source, source ^ mask) for source in range(lax.axis_size("blk"))]
    return lax.ppermute(value, "blk", pairs)


def rms_round(hidden, gain):
    values = hidden.astype(jnp.float32)
    meansq = jnp.mean(values * values, axis=-1, keepdims=True)
    return (values * lax.rsqrt(meansq + 1e-06) * gain).astype(jnp.bfloat16)


def cost(micros):
    return pl.CostEstimate(flops=int(micros * 1e9), bytes_accessed=int(micros * 3e6), transcendentals=0)


def iota(shape, dim):
    return lax.broadcasted_iota(jnp.int32, shape, dim)


def dot(a, b, dims, precision=None):
    return lax.dot_general(a, b, dims, precision=precision, preferred_element_type=F32)


def attend_kernel(
    perm_h, lengths_h, queries_h, new_h, cache, w_uv, out,
    perm, lengths, queries, new_kv, qs, keys, up, sems, others,
):
    slots, width, positions = cache.shape
    heads, latent, nope = w_uv.shape
    rows = heads * slots
    first = lax.axis_index("blk") * slots
    small = [
        pltpu.make_async_copy(source, target, others.at[k])
        for k, (source, target) in enumerate(
            ((queries_h, queries), (new_h, new_kv), (perm_h, perm), (lengths_h, lengths))
        )
    ]
    copies = [
        pltpu.make_async_copy(cache.at[s], keys.at[s], sems.at[s]) for s in range(slots)
    ]
    upcopy = pltpu.make_async_copy(w_uv, up, others.at[4])
    for copy in small + copies + [upcopy]:
        copy.start()
    small[0].wait()
    for h in range(heads):
        qs[h * slots : (h + 1) * slots, :] = queries[:, h * width : (h + 1) * width]
    q = qs[...]
    small[1].wait()
    new = new_kv[...]
    scale = (nope + width - latent) ** (-0.5)
    slot_of = iota((rows, 1), 0) % slots
    own = dot(q, new, NT)
    own = jnp.sum(jnp.where(iota((rows, slots), 1) == slot_of, own, 0.0), 1, keepdims=True) * scale
    small[2].wait()
    small[3].wait()
    live = jnp.zeros((rows, 1), jnp.int32)
    for s in range(slots):
        live = jnp.where(slot_of == s, lengths[0, perm[first + s]], live)
    scores = jnp.zeros((rows, positions), F32)
    for s in range(slots):
        copies[s].wait()
        scores = jnp.where(slot_of == s, dot(q, keys[s], NN), scores)
    mask = iota((rows, positions), 1) < live
    scores = jnp.where(mask, scores * scale, -1e30)
    peak = jnp.maximum(jnp.max(scores, axis=1, keepdims=True), own)
    probs = jnp.where(mask, jnp.exp(scores - peak), 0.0)
    own = jnp.exp(own - peak)
    total = jnp.sum(probs, axis=1, keepdims=True) + own
    weights = probs / total
    own = (own / total).astype(BF).astype(F32)
    mixed = jnp.zeros((rows, latent), F32)
    for s in range(slots):
        part = jnp.where(slot_of == s, weights, 0.0).astype(BF)
        mixed += dot(part, keys[s, :latent, :], NT)
    mixed += own * jnp.tile(new[:, :latent].astype(F32), (heads, 1))
    upcopy.wait()
    for h in range(heads):
        rows_h = mixed[h * slots : (h + 1) * slots, :].astype(BF)
        out[:, h * nope : (h + 1) * nope] = dot(rows_h, up[h], NN).astype(BF)


def attend(perm, lengths, queries, new_kv, cache, w_uv):
    slots, width, positions = cache.shape
    heads, latent, nope = w_uv.shape
    return pl.pallas_call(
        attend_kernel,
        out_shape=jax.ShapeDtypeStruct((slots, heads * nope), BF),
        in_specs=[HB] * 6,
        out_specs=VM,
        scratch_shapes=[
            pltpu.SMEM(perm.shape, jnp.int32),
            pltpu.SMEM(lengths.shape, jnp.int32),
            pltpu.VMEM(queries.shape, BF),
            pltpu.VMEM(new_kv.shape, BF),
            pltpu.VMEM((heads * slots, width), BF),
            pltpu.VMEM((slots, width, positions), BF),
            pltpu.VMEM((heads, latent, nope), BF),
            pltpu.SemaphoreType.DMA((slots,)),
            pltpu.SemaphoreType.DMA((5,)),
        ],
        compiler_params=pltpu.CompilerParams(vmem_limit_bytes=60 << 20),
        cost_estimate=cost(15),
        name="attend",
    )(perm, lengths, queries, new_kv, cache, w_uv)


def request_of(row, rows):
    chip = ((row >> 2) & 3) * 4 + (row >> 5)
    return ((row >> 4) & 1) * (rows // 2) + chip * 4 + (row & 3)


def project_kernel(perm, v0, v1, v2, v3, w_out, x_cols, out, full):
    blk = lax.axis_index("blk")
    rows = x_cols.shape[0]
    part = v0.shape[0]
    for q, ref in enumerate((v0, v1, v2, v3)):
        full[q * part : (q + 1) * part, :] = ref[...]
    attended = dot(full[...], w_out[...], NN)
    shape = (rows, rows)
    wanted = request_of(iota(shape, 0), rows)
    by_slot = (jnp.broadcast_to(perm[...], shape) == wanted).astype(F32)
    arrived = iota(shape, 1)
    slot = ((blk ^ (((arrived >> 3) & 3) * 4) ^ (arrived >> 5)) << 3) | (arrived & 7)
    move = (iota(shape, 0) == slot).astype(F32)
    by_arrival = dot(by_slot.astype(BF), move.astype(BF), NN)
    moved = dot(by_arrival, attended, NN, lax.Precision.HIGHEST)
    base = dot(by_slot.astype(BF), x_cols[...], NN)
    out[...] = (base + moved).astype(BF)


def project(perm, pieces, w_out, x_cols):
    return pl.pallas_call(
        project_kernel,
        out_shape=jax.ShapeDtypeStruct(x_cols.shape, BF),
        in_specs=[VM] * 7,
        out_specs=VM,
        scratch_shapes=[pltpu.VMEM((x_cols.shape[0], w_out.shape[0]), BF)],
        compiler_params=pltpu.CompilerParams(vmem_limit_bytes=4 << 20),
        cost_estimate=cost(15),
        name="project",
    )(perm, *pieces, w_out, x_cols)


def feed_kernel(
    r0, r1, r2, r3, gain, w_gate, w_up, w_down, own, c1, c2, c3, kept, full, acc
):
    blk = lax.axis_index("blk")
    groups, rows, cols = r0.shape
    units = w_gate.shape[0]
    for q, ref in enumerate((r0, r1, r2, r3)):
        for j in range(groups):
            at = pl.multiple_of((blk ^ (4 * j) ^ q) * cols, cols)
            full[:, pl.ds(at, cols)] = ref[j].astype(F32)
    values = full[...]
    meansq = jnp.mean(values * values, axis=1, keepdims=True)
    normed = (values * lax.rsqrt(meansq + 1e-06) * gain[...]).astype(BF)
    gate = dot(normed, w_gate[...], NT)
    up = dot(normed, w_up[...], NT)
    unit = blk * units + iota((rows, units), 1)
    hidden = gate * (1.0 / (1.0 + jnp.exp(-gate))) * up
    hidden = jnp.where(unit < FF, hidden, 0.0).astype(BF)
    acc[...] = dot(hidden, w_down[...], NN)
    low = blk & 3
    chunk = rows // 4
    for q, ref in enumerate((own, c1, c2, c3)):
        at = pl.multiple_of((low ^ q) * chunk, chunk)
        ref[...] = acc[pl.ds(at, chunk), :].astype(ref.dtype)
    kept[...] = full[pl.ds(pl.multiple_of(low * chunk, chunk), chunk), :]


def feed(pieces, gain, w_gate, w_up, w_down):
    groups, rows, cols = pieces[0].shape
    width = w_down.shape[1]
    part = (rows // 4, width)
    return pl.pallas_call(
        feed_kernel,
        out_shape=[
            jax.ShapeDtypeStruct(part, F32),
            jax.ShapeDtypeStruct(part, BF),
            jax.ShapeDtypeStruct(part, BF),
            jax.ShapeDtypeStruct(part, BF),
            jax.ShapeDtypeStruct(part, F32),
        ],
        in_specs=[VM] * 8,
        out_specs=[VM] * 5,
        scratch_shapes=[pltpu.VMEM((rows, width), F32), pltpu.VMEM((rows, width), F32)],
        compiler_params=pltpu.CompilerParams(vmem_limit_bytes=8 << 20),
        cost_estimate=cost(15),
        name="feed",
    )(*pieces, gain, w_gate, w_up, w_down)


def sum_kernel(*refs):
    out = refs[-1]
    total = refs[0][...].astype(F32)
    for ref in refs[1:-1]:
        total += ref[...].astype(F32)
    out[...] = total.astype(out.dtype)


def add(parts):
    return pl.pallas_call(
        sum_kernel,
        out_shape=jax.ShapeDtypeStruct(parts[0].shape, BF),
        in_specs=[VM] * len(parts),
        out_specs=VM,
        compiler_params=pltpu.CompilerParams(vmem_limit_bytes=2 << 20),
        cost_estimate=cost(20),
        name="add",
    )(*parts)


def finish_kernel(own, other, kept, gain, stay, go):
    after = (kept[...] + (own[...].astype(F32) + other[...].astype(F32))).astype(BF).astype(F32)
    meansq = jnp.mean(after * after, axis=1, keepdims=True)
    normed = (after * lax.rsqrt(meansq + 1e-06) * gain[...]).astype(BF)
    half = normed.shape[0] // 2
    first, last = normed[:half], normed[half:]
    lower = lax.axis_index("guide") == 0
    stay[...] = jnp.where(lower, first, last)
    go[...] = jnp.where(lower, last, first)


def finish(own, other, kept, gain):
    rows, width = own.shape
    return pl.pallas_call(
        finish_kernel,
        out_shape=[jax.ShapeDtypeStruct((rows // 2, width), BF)] * 2,
        in_specs=[VM] * 4,
        out_specs=[VM] * 2,
        compiler_params=pltpu.CompilerParams(vmem_limit_bytes=2 << 20),
        cost_estimate=cost(20),
        name="finish",
    )(own, other, kept, gain)


def head_kernel(r0, r1, r2, r3, scale, w_head, out, came, full, factor, done, sems):
    guide, blk = lax.axis_index("guide"), lax.axis_index("blk")
    part = r0.shape[0]
    rows = 4 * part
    half = rows // 2
    tiles, _, tile = done.shape
    for q, ref in enumerate((r0, r1, r2, r3)):
        came[q * part : (q + 1) * part, :] = ref[...]
    at = iota((rows, rows), 1)
    chip = (((at >> 2) & 3) << 2) + ((blk & 3) ^ (at >> 5))
    row = (((at >> 4) & 1) ^ guide) * half + chip * 4 + (at & 3)
    order = (row == iota((rows, rows), 0)).astype(BF)
    full[...] = dot(order, came[...], NN).astype(BF)
    mine = iota((half, rows), 0) + guide * half == iota((half, rows), 1)
    factor[...] = jnp.sum(
        jnp.where(mine, jnp.broadcast_to(scale[...], (half, rows)), 0.0), 1, keepdims=True
    )

    def store(step):
        at = pl.ds(pl.multiple_of(step * tile, tile), tile)
        return pltpu.make_async_copy(done.at[step], out.at[:, at], sems.at[step])

    @pl.loop(0, tiles)
    def _(step):
        at = pl.ds(pl.multiple_of(step * tile, tile), tile)
        logits = dot(full[...], w_head[:, at], NN)
        cond, uncond = logits[:half], logits[half:]
        done[step] = (uncond + factor[...] * (cond - uncond)).astype(BF)
        store(step).start()

    @pl.loop(0, tiles)
    def _(step):
        store(step).wait()


def head(pieces, scale, w_head):
    part, width = pieces[0].shape
    rows = 4 * part
    vocab = w_head.shape[1]
    tile = next(t for t in (1280, 256, 128) if vocab % t == 0)
    return pl.pallas_call(
        head_kernel,
        out_shape=jax.ShapeDtypeStruct((rows // 2, vocab), BF),
        in_specs=[VM] * 6,
        out_specs=HB,
        scratch_shapes=[
            pltpu.VMEM((rows, width), BF),
            pltpu.VMEM((rows, width), BF),
            pltpu.VMEM((rows // 2, 1), F32),
            pltpu.VMEM((vocab // tile, rows // 2, tile), BF),
            pltpu.SemaphoreType.DMA((vocab // tile,)),
        ],
        compiler_params=pltpu.CompilerParams(vmem_limit_bytes=8 << 20),
        cost_estimate=cost(8),
        name="head",
    )(*pieces, scale, w_head)


def join_kernel(*refs):
    out = refs[-1]
    part = refs[0].shape[0]
    for k, ref in enumerate(refs[:-1]):
        out[k * part : (k + 1) * part, :] = ref[...]


def join(parts):
    rows, width = parts[0].shape
    return pl.pallas_call(
        join_kernel,
        out_shape=jax.ShapeDtypeStruct((len(parts) * rows, width), parts[0].dtype),
        in_specs=[VM] * len(parts),
        out_specs=VM,
        compiler_params=pltpu.CompilerParams(vmem_limit_bytes=1 << 20),
        cost_estimate=cost(1),
        name="join",
    )(*parts)


def spread(value):
    group = join([value] + [swap(value, mask) for mask in (4, 8, 12)])
    return [group] + [swap(group, mask) for mask in (1, 2, 3)]


def fast_body(
    x_cols,
    queries,
    new_kv,
    cache,
    lengths,
    perm,
    guide_scale,
    w_uv,
    w_out,
    mlp_gain,
    w_gate,
    w_up,
    w_down,
    head_gain,
    w_head,
):
    rows, cols = x_cols.shape
    keys = jnp.swapaxes(cache[0], 1, 2)
    values = attend(perm, lengths, queries, new_kv, keys, w_uv)
    residual = project(perm[None], spread(values), w_out, x_cols)
    pieces = [piece.reshape(4, rows, cols) for piece in spread(residual)]
    own, *chunks, kept = feed(
        pieces, mlp_gain[None], jnp.swapaxes(w_gate, 0, 1), jnp.swapaxes(w_up, 0, 1), w_down
    )
    arrived = [swap(chunk, mask) for chunk, mask in zip(chunks, (1, 2, 3))]
    part = add([own] + arrived)
    part = add([part, swap(part, 4)])
    stay, go = finish(part, swap(part, 8), kept, head_gain[None])
    normed = join([stay, partner(go, "guide", 0)])
    return head([normed] + [swap(normed, mask) for mask in (1, 2, 3)], guide_scale[None], w_head)


def body(
    x_cols,
    queries,
    new_kv,
    cache,
    lengths,
    perm,
    guide_scale,
    w_uv,
    w_out,
    mlp_gain,
    w_gate,
    w_up,
    w_down,
    head_gain,
    w_head,
):
    guide_index = lax.axis_index("guide")
    blk_index = lax.axis_index("blk")
    slots_dev = queries.shape[0]
    heads_count = w_uv.shape[0]
    latent_size = w_uv.shape[1]
    key_width = new_kv.shape[1]
    score_scale = (w_uv.shape[2] + key_width - latent_size) ** (-0.5)
    slot_ids = blk_index * slots_dev + jnp.arange(slots_dev, dtype=jnp.int32)
    owners = jnp.take(perm, slot_ids)
    live_len = jnp.take(lengths[0], owners)
    query_heads = queries.reshape(slots_dev, heads_count, key_width)
    cached_keys = cache[0]
    scores = (
        jnp.einsum("shk,slk->shl", query_heads, cached_keys, preferred_element_type=jnp.float32)
        * score_scale
    )
    own_score = (
        jnp.einsum("shk,sk->sh", query_heads, new_kv, preferred_element_type=jnp.float32)
        * score_scale
    )
    live_mask = (
        jnp.arange(cached_keys.shape[1], dtype=jnp.int32)[None, None, :] < live_len[:, None, None]
    )
    scores = jnp.where(live_mask, scores, jnp.float32(-1e30))
    peak_score = jnp.maximum(jnp.max(scores, axis=-1), own_score)
    probs = jnp.where(live_mask, jnp.exp(scores - peak_score[..., None]), jnp.float32(0.0))
    own_prob = jnp.exp(own_score - peak_score)
    softmax_total = jnp.sum(probs, axis=-1) + own_prob
    weights = (probs / softmax_total[..., None]).astype(jnp.bfloat16)
    own_weight = (own_prob / softmax_total).astype(jnp.bfloat16)
    latent_out = jnp.einsum(
        "shl,slc->shc", weights, cached_keys[:, :, :latent_size], preferred_element_type=jnp.float32
    )
    latent_out = latent_out + own_weight.astype(jnp.float32)[..., None] * new_kv[
        :, None, :latent_size
    ].astype(jnp.float32)
    value_rows = jnp.einsum(
        "shc,hcd->shd", latent_out.astype(jnp.bfloat16), w_uv, preferred_element_type=jnp.float32
    )
    value_rows = value_rows.astype(jnp.bfloat16).reshape(slots_dev, -1)
    attended = jnp.dot(
        lax.all_gather(value_rows, "blk", axis=0, tiled=True),
        w_out,
        preferred_element_type=jnp.float32,
    )
    residual = (x_cols.astype(jnp.float32) + attended).astype(jnp.bfloat16)
    rows_full = lax.all_gather(residual, "blk", axis=1, tiled=True)
    normed = rms_round(rows_full, mlp_gain)
    unit_count = w_gate.shape[1]
    gate_out = jnp.dot(normed, w_gate, preferred_element_type=jnp.float32)
    up_out = jnp.dot(normed, w_up, preferred_element_type=jnp.float32)
    unit_ids = blk_index * unit_count + jnp.arange(unit_count, dtype=jnp.int32)
    hidden = jnp.where(
        unit_ids[None, :] < FF, jax.nn.silu(gate_out) * up_out, jnp.float32(0.0)
    ).astype(jnp.bfloat16)
    partial_sum = jnp.dot(hidden, w_down, preferred_element_type=jnp.float32)
    summed = lax.psum(partial_sum, "blk")
    after_mlp = (rows_full.astype(jnp.float32) + summed).astype(jnp.bfloat16)
    logits = jnp.dot(rms_round(after_mlp, head_gain), w_head, preferred_element_type=jnp.float32)
    request_count = logits.shape[0]
    half_rows = request_count // 2
    slot_scale = jnp.take(guide_scale, perm)
    request_order = (
        jnp.zeros((request_count,), jnp.int32)
        .at[perm]
        .set(jnp.arange(request_count, dtype=jnp.int32))
    )
    own_order = lax.dynamic_slice_in_dim(request_order, guide_index * half_rows, half_rows)
    other_logits = partner(logits.astype(jnp.bfloat16), "guide", 0).astype(logits.dtype)
    cond_logits = jnp.where(guide_index == 0, logits, other_logits)
    uncond_logits = jnp.where(guide_index == 0, other_logits, logits)
    mixed = (uncond_logits + slot_scale[:, None] * (cond_logits - uncond_logits)).astype(
        jnp.bfloat16
    )
    return jnp.take(mixed, own_order, axis=0)


def solution(mesh):
    def run(*args):
        chips = mesh.shape["blk"]
        rows, width = args[0].shape
        fits = chips == 16 and rows == 128 and mesh.shape["guide"] == 2 and width % (128 * chips) == 0
        return jax.shard_map(
            fast_body if fits else body,
            mesh=mesh,
            in_specs=(
                P(None, "blk"),
                P("blk", None),
                P("blk", None),
                P("guide", "blk", None, None),
                P("guide", None),
                P(),
                P(),
                P(),
                P(None, "blk"),
                P(),
                P(None, "blk"),
                P(None, "blk"),
                P("blk", None),
                P(),
                P(None, "blk"),
            ),
            out_specs=P("guide", "blk"),
            check_vma=False,
        )(*args)

    return run
```

```python
import jax
import jax.numpy as jnp
from jax import lax
from jax.experimental import pallas as pl
from jax.experimental.pallas import tpu as pltpu
from jax.sharding import PartitionSpec as P

FF = 10944
BF = jnp.bfloat16
F32 = jnp.float32
NN = (((1,), (0,)), ((), ()))
NT = (((1,), (1,)), ((), ()))
TN = (((0,), (0,)), ((), ()))
VM = pl.BlockSpec(memory_space=pltpu.VMEM)
HB = pl.BlockSpec(memory_space=pltpu.HBM)


def across(value, mask):
    chips = lax.axis_size("blk")
    pairs = [(d, (d ^ mask) ^ chips) for d in range(2 * chips)]
    return lax.ppermute(value, ("guide", "blk"), pairs)


def partner(value, axis, apart):
    mask = 2**apart
    pairs = [(source, source ^ mask) for source in range(lax.axis_size(axis))]
    return lax.ppermute(value, axis, pairs)


def swap(value, mask):
    pairs = [(source, source ^ mask) for source in range(lax.axis_size("blk"))]
    return lax.ppermute(value, "blk", pairs)


def rms_round(hidden, gain):
    values = hidden.astype(jnp.float32)
    meansq = jnp.mean(values * values, axis=-1, keepdims=True)
    return (values * lax.rsqrt(meansq + 1e-06) * gain).astype(jnp.bfloat16)


def cost(micros):
    return pl.CostEstimate(flops=int(micros * 1e9), bytes_accessed=int(micros * 3e6), transcendentals=0)


def iota(shape, dim):
    return lax.broadcasted_iota(jnp.int32, shape, dim)


def dot(a, b, dims, precision=None):
    return lax.dot_general(a, b, dims, precision=precision, preferred_element_type=F32)


def attend_kernel(
    perm_h, lengths_h, queries_h, new_h, cache, w_uv, out,
    perm, lengths, queries, new_kv, qs, keys, up, sems, others,
):
    slots, width, positions = cache.shape
    heads, latent, nope = w_uv.shape
    rows = heads * slots
    first = lax.axis_index("blk") * slots
    small = [
        pltpu.make_async_copy(source, target, others.at[k])
        for k, (source, target) in enumerate(
            ((queries_h, queries), (new_h, new_kv), (perm_h, perm), (lengths_h, lengths))
        )
    ]
    copies = [
        pltpu.make_async_copy(cache.at[s], keys.at[s], sems.at[s]) for s in range(slots)
    ]
    upcopy = pltpu.make_async_copy(w_uv, up, others.at[4])
    for copy in small + copies + [upcopy]:
        copy.start()
    small[0].wait()
    for h in range(heads):
        qs[h * slots : (h + 1) * slots, :] = queries[:, h * width : (h + 1) * width]
    q = qs[...]
    small[1].wait()
    new = new_kv[...]
    scale = (nope + width - latent) ** (-0.5)
    slot_of = iota((rows, 1), 0) % slots
    own = dot(q, new, NT)
    own = jnp.sum(jnp.where(iota((rows, slots), 1) == slot_of, own, 0.0), 1, keepdims=True) * scale
    small[2].wait()
    small[3].wait()
    live = jnp.zeros((rows, 1), jnp.int32)
    for s in range(slots):
        live = jnp.where(slot_of == s, lengths[0, perm[first + s]], live)
    for copy in copies:
        copy.wait()
    scores = jnp.zeros((rows, positions), F32)
    for s in range(slots):
        scores = jnp.where(slot_of == s, dot(q, keys[s], NN), scores)
    mask = iota((rows, positions), 1) < live
    scores = jnp.where(mask, scores * scale, -1e30)
    peak = jnp.maximum(jnp.max(scores, axis=1, keepdims=True), own)
    probs = jnp.where(mask, jnp.exp(scores - peak), 0.0)
    own = jnp.exp(own - peak)
    total = jnp.sum(probs, axis=1, keepdims=True) + own
    weights = probs / total
    own = (own / total).astype(BF).astype(F32)
    mixed = jnp.zeros((rows, latent), F32)
    for s in range(slots):
        part = jnp.where(slot_of == s, weights, 0.0).astype(BF)
        mixed += dot(part, keys[s, :latent, :], NT)
    mixed += own * jnp.tile(new[:, :latent].astype(F32), (heads, 1))
    upcopy.wait()
    for h in range(heads):
        rows_h = mixed[h * slots : (h + 1) * slots, :].astype(BF)
        out[:, h * nope : (h + 1) * nope] = dot(rows_h, up[h], NN).astype(BF)


def attend(perm, lengths, queries, new_kv, cache, w_uv):
    slots, width, positions = cache.shape
    heads, latent, nope = w_uv.shape
    return pl.pallas_call(
        attend_kernel,
        out_shape=jax.ShapeDtypeStruct((slots, heads * nope), BF),
        in_specs=[HB] * 6,
        out_specs=VM,
        scratch_shapes=[
            pltpu.SMEM(perm.shape, jnp.int32),
            pltpu.SMEM(lengths.shape, jnp.int32),
            pltpu.VMEM(queries.shape, BF),
            pltpu.VMEM(new_kv.shape, BF),
            pltpu.VMEM((heads * slots, width), BF),
            pltpu.VMEM((slots, width, positions), BF),
            pltpu.VMEM((heads, latent, nope), BF),
            pltpu.SemaphoreType.DMA((slots,)),
            pltpu.SemaphoreType.DMA((5,)),
        ],
        compiler_params=pltpu.CompilerParams(vmem_limit_bytes=60 << 20),
        cost_estimate=cost(15),
        name="attend",
    )(perm, lengths, queries, new_kv, cache, w_uv)


def request_of(row, rows):
    chip = ((row >> 2) & 3) * 4 + (row >> 5)
    return ((row >> 4) & 1) * (rows // 2) + chip * 4 + (row & 3)


def project_kernel(perm, v0, v1, v2, v3, w_out, x_cols, out, full):
    blk = lax.axis_index("blk")
    rows = x_cols.shape[0]
    part = v0.shape[0]
    for q, ref in enumerate((v0, v1, v2, v3)):
        full[q * part : (q + 1) * part, :] = ref[...]
    attended = dot(full[...], w_out[...], NN)
    shape = (rows, rows)
    wanted = request_of(iota(shape, 0), rows)
    by_slot = (jnp.broadcast_to(perm[...], shape) == wanted).astype(F32)
    arrived = iota(shape, 1)
    slot = ((blk ^ (((arrived >> 3) & 3) * 4) ^ (arrived >> 5)) << 3) | (arrived & 7)
    move = (iota(shape, 0) == slot).astype(F32)
    by_arrival = dot(by_slot.astype(BF), move.astype(BF), NN)
    moved = dot(by_arrival, attended, NN, lax.Precision.HIGHEST)
    base = dot(by_slot.astype(BF), x_cols[...], NN)
    out[...] = (base + moved).astype(BF)


def project(perm, pieces, w_out, x_cols):
    return pl.pallas_call(
        project_kernel,
        out_shape=jax.ShapeDtypeStruct(x_cols.shape, BF),
        in_specs=[VM] * 7,
        out_specs=VM,
        scratch_shapes=[pltpu.VMEM((x_cols.shape[0], w_out.shape[0]), BF)],
        compiler_params=pltpu.CompilerParams(vmem_limit_bytes=4 << 20),
        cost_estimate=cost(15),
        name="project",
    )(perm, *pieces, w_out, x_cols)


def feed_kernel(
    r0, r1, r2, r3, gain, w_gate, w_up, w_down, own, c1, c2, c3, stay, go, full, acc
):
    blk = lax.axis_index("blk")
    groups, rows, cols = r0.shape
    units = w_gate.shape[0]
    for q, ref in enumerate((r0, r1, r2, r3)):
        for j in range(groups):
            at = pl.multiple_of((blk ^ (4 * j) ^ q) * cols, cols)
            full[:, pl.ds(at, cols)] = ref[j].astype(F32)
    values = full[...]
    meansq = jnp.mean(values * values, axis=1, keepdims=True)
    normed = (values * lax.rsqrt(meansq + 1e-06) * gain[...]).astype(BF)
    gate = dot(normed, w_gate[...], NT)
    up = dot(normed, w_up[...], NT)
    unit = blk * units + iota((rows, units), 1)
    hidden = gate * (1.0 / (1.0 + jnp.exp(-gate))) * up
    hidden = jnp.where(unit < FF, hidden, 0.0).astype(BF)
    acc[...] = dot(hidden, w_down[...], NN)
    low = blk & 3
    chunk = rows // 4
    for q, ref in enumerate((own, c1, c2, c3)):
        at = pl.multiple_of((low ^ q) * chunk, chunk)
        ref[...] = acc[pl.ds(at, chunk), :].astype(ref.dtype)
    first = full[pl.ds(pl.multiple_of(low * chunk, chunk), chunk // 2), :]
    last = full[pl.ds(pl.multiple_of(low * chunk + chunk // 2, chunk // 2), chunk // 2), :]
    lower = lax.axis_index("guide") == 0
    stay[...] = jnp.where(lower, first, last).astype(BF)
    go[...] = jnp.where(lower, last, first).astype(BF)


def feed(pieces, gain, w_gate, w_up, w_down):
    groups, rows, cols = pieces[0].shape
    width = w_down.shape[1]
    part = (rows // 4, width)
    return pl.pallas_call(
        feed_kernel,
        out_shape=[
            jax.ShapeDtypeStruct(part, F32),
            jax.ShapeDtypeStruct(part, BF),
            jax.ShapeDtypeStruct(part, BF),
            jax.ShapeDtypeStruct(part, BF),
            jax.ShapeDtypeStruct((rows // 8, width), BF),
            jax.ShapeDtypeStruct((rows // 8, width), BF),
        ],
        in_specs=[VM] * 8,
        out_specs=[VM] * 6,
        scratch_shapes=[pltpu.VMEM((rows, width), F32), pltpu.VMEM((rows, width), F32)],
        compiler_params=pltpu.CompilerParams(vmem_limit_bytes=8 << 20),
        cost_estimate=cost(15),
        name="feed",
    )(*pieces, gain, w_gate, w_up, w_down)


def part_kernel(own, p1, p2, p3, stay, go):
    total = own[...] + p1[...].astype(F32) + p2[...].astype(F32) + p3[...].astype(F32)
    half = total.shape[0] // 2
    first, last = total[:half], total[half:]
    lower = lax.axis_index("guide") == 0
    stay[...] = jnp.where(lower, first, last).astype(BF)
    go[...] = jnp.where(lower, last, first).astype(BF)


def pair_kernel(a, b, c, d, out):
    half = a.shape[0]
    out[:half, :] = (a[...].astype(F32) + b[...].astype(F32)).astype(BF)
    out[half:, :] = (c[...].astype(F32) + d[...].astype(F32)).astype(BF)


def finish_kernel(own, other, stay, came, gain, out):
    half = stay.shape[0]
    total = own[...].astype(F32) + other[...].astype(F32)
    for k, ref in enumerate((stay, came)):
        at = slice(k * half, (k + 1) * half)
        after = (ref[...].astype(F32) + total[at]).astype(BF).astype(F32)
        meansq = jnp.mean(after * after, axis=1, keepdims=True)
        out[at, :] = (after * lax.rsqrt(meansq + 1e-06) * gain[...]).astype(BF)


def small(kernel, name, shapes, *args):
    return pl.pallas_call(
        kernel,
        out_shape=[jax.ShapeDtypeStruct(shape, BF) for shape in shapes],
        in_specs=[VM] * len(args),
        out_specs=[VM] * len(shapes),
        compiler_params=pltpu.CompilerParams(vmem_limit_bytes=2 << 20),
        cost_estimate=cost(20),
        name=name,
    )(*args)


def head_kernel(r0, r1, r2, r3, scale, w_head, out, came, full, factor, done, sems):
    guide, blk = lax.axis_index("guide"), lax.axis_index("blk")
    part = r0.shape[0]
    rows = 4 * part
    half = rows // 2
    tiles, _, tile = done.shape
    for q, ref in enumerate((r0, r1, r2, r3)):
        came[q * part : (q + 1) * part, :] = ref[...]
    at = iota((rows, rows), 1)
    chip = (((at >> 2) & 3) << 2) + ((blk & 3) ^ (at >> 5))
    row = (((at >> 4) & 1) ^ guide) * half + chip * 4 + (at & 3)
    order = (row == iota((rows, rows), 0)).astype(BF)
    full[...] = dot(order, came[...], NN).astype(BF)
    mine = iota((half, rows), 0) + guide * half == iota((half, rows), 1)
    factor[...] = jnp.sum(
        jnp.where(mine, jnp.broadcast_to(scale[...], (half, rows)), 0.0), 1, keepdims=True
    )

    def store(step):
        at = pl.ds(pl.multiple_of(step * tile, tile), tile)
        return pltpu.make_async_copy(done.at[step], out.at[:, at], sems.at[step])

    @pl.loop(0, tiles)
    def _(step):
        at = pl.ds(pl.multiple_of(step * tile, tile), tile)
        logits = dot(full[...], w_head[:, at], NN)
        cond, uncond = logits[:half], logits[half:]
        done[step] = (uncond + factor[...] * (cond - uncond)).astype(BF)
        store(step).start()

    @pl.loop(0, tiles)
    def _(step):
        store(step).wait()


def head(pieces, scale, w_head):
    part, width = pieces[0].shape
    rows = 4 * part
    vocab = w_head.shape[1]
    tile = next(t for t in (1280, 256, 128) if vocab % t == 0)
    return pl.pallas_call(
        head_kernel,
        out_shape=jax.ShapeDtypeStruct((rows // 2, vocab), BF),
        in_specs=[VM] * 6,
        out_specs=HB,
        scratch_shapes=[
            pltpu.VMEM((rows, width), BF),
            pltpu.VMEM((rows, width), BF),
            pltpu.VMEM((rows // 2, 1), F32),
            pltpu.VMEM((vocab // tile, rows // 2, tile), BF),
            pltpu.SemaphoreType.DMA((vocab // tile,)),
        ],
        compiler_params=pltpu.CompilerParams(vmem_limit_bytes=8 << 20),
        cost_estimate=cost(8),
        name="head",
    )(*pieces, scale, w_head)


def join_kernel(*refs):
    out = refs[-1]
    part = refs[0].shape[0]
    for k, ref in enumerate(refs[:-1]):
        out[k * part : (k + 1) * part, :] = ref[...]


def join(parts):
    rows, width = parts[0].shape
    return pl.pallas_call(
        join_kernel,
        out_shape=jax.ShapeDtypeStruct((len(parts) * rows, width), parts[0].dtype),
        in_specs=[VM] * len(parts),
        out_specs=VM,
        compiler_params=pltpu.CompilerParams(vmem_limit_bytes=1 << 20),
        cost_estimate=cost(1),
        name="join",
    )(*parts)


def spread(value, own):
    group = join([own] + [swap(value, mask) for mask in (4, 8, 12)])
    return [group] + [swap(group, mask) for mask in (1, 2, 3)]


def fast_body(
    x_cols,
    queries,
    new_kv,
    cache,
    lengths,
    perm,
    guide_scale,
    w_uv,
    w_out,
    mlp_gain,
    w_gate,
    w_up,
    w_down,
    head_gain,
    w_head,
):
    rows, cols = x_cols.shape
    keys = jnp.swapaxes(cache[0], 1, 2)
    values = attend(perm, lengths, queries, new_kv, keys, w_uv)
    residual = project(perm[None], spread(values, join([values])), w_out, x_cols)
    pieces = [piece.reshape(4, rows, cols) for piece in spread(residual, residual)]
    own, *chunks, stay, go = feed(
        pieces, mlp_gain[None], jnp.swapaxes(w_gate, 0, 1), jnp.swapaxes(w_up, 0, 1), w_down
    )
    came = partner(go, "guide", 0)
    arrived = [swap(chunk, mask) for chunk, mask in zip(chunks, (1, 2, 3))]
    came, arrived[0] = lax.optimization_barrier((came, arrived[0]))
    half, part = stay.shape, own.shape
    mine, his = small(part_kernel, "part", (half, half), own, *arrived)
    sums = (mine, swap(mine, 4), partner(his, "guide", 0), across(his, 4))
    (total,) = small(pair_kernel, "pair", (part,), *sums)
    (normed,) = small(
        finish_kernel, "finish", (part,), total, swap(total, 8), stay, came, head_gain[None]
    )
    return head([normed] + [swap(normed, mask) for mask in (1, 2, 3)], guide_scale[None], w_head)


def body(
    x_cols,
    queries,
    new_kv,
    cache,
    lengths,
    perm,
    guide_scale,
    w_uv,
    w_out,
    mlp_gain,
    w_gate,
    w_up,
    w_down,
    head_gain,
    w_head,
):
    guide_index = lax.axis_index("guide")
    blk_index = lax.axis_index("blk")
    slots_dev = queries.shape[0]
    heads_count = w_uv.shape[0]
    latent_size = w_uv.shape[1]
    key_width = new_kv.shape[1]
    score_scale = (w_uv.shape[2] + key_width - latent_size) ** (-0.5)
    slot_ids = blk_index * slots_dev + jnp.arange(slots_dev, dtype=jnp.int32)
    owners = jnp.take(perm, slot_ids)
    live_len = jnp.take(lengths[0], owners)
    query_heads = queries.reshape(slots_dev, heads_count, key_width)
    cached_keys = cache[0]
    scores = (
        jnp.einsum("shk,slk->shl", query_heads, cached_keys, preferred_element_type=jnp.float32)
        * score_scale
    )
    own_score = (
        jnp.einsum("shk,sk->sh", query_heads, new_kv, preferred_element_type=jnp.float32)
        * score_scale
    )
    live_mask = (
        jnp.arange(cached_keys.shape[1], dtype=jnp.int32)[None, None, :] < live_len[:, None, None]
    )
    scores = jnp.where(live_mask, scores, jnp.float32(-1e30))
    peak_score = jnp.maximum(jnp.max(scores, axis=-1), own_score)
    probs = jnp.where(live_mask, jnp.exp(scores - peak_score[..., None]), jnp.float32(0.0))
    own_prob = jnp.exp(own_score - peak_score)
    softmax_total = jnp.sum(probs, axis=-1) + own_prob
    weights = (probs / softmax_total[..., None]).astype(jnp.bfloat16)
    own_weight = (own_prob / softmax_total).astype(jnp.bfloat16)
    latent_out = jnp.einsum(
        "shl,slc->shc", weights, cached_keys[:, :, :latent_size], preferred_element_type=jnp.float32
    )
    latent_out = latent_out + own_weight.astype(jnp.float32)[..., None] * new_kv[
        :, None, :latent_size
    ].astype(jnp.float32)
    value_rows = jnp.einsum(
        "shc,hcd->shd", latent_out.astype(jnp.bfloat16), w_uv, preferred_element_type=jnp.float32
    )
    value_rows = value_rows.astype(jnp.bfloat16).reshape(slots_dev, -1)
    attended = jnp.dot(
        lax.all_gather(value_rows, "blk", axis=0, tiled=True),
        w_out,
        preferred_element_type=jnp.float32,
    )
    residual = (x_cols.astype(jnp.float32) + attended).astype(jnp.bfloat16)
    rows_full = lax.all_gather(residual, "blk", axis=1, tiled=True)
    normed = rms_round(rows_full, mlp_gain)
    unit_count = w_gate.shape[1]
    gate_out = jnp.dot(normed, w_gate, preferred_element_type=jnp.float32)
    up_out = jnp.dot(normed, w_up, preferred_element_type=jnp.float32)
    unit_ids = blk_index * unit_count + jnp.arange(unit_count, dtype=jnp.int32)
    hidden = jnp.where(
        unit_ids[None, :] < FF, jax.nn.silu(gate_out) * up_out, jnp.float32(0.0)
    ).astype(jnp.bfloat16)
    partial_sum = jnp.dot(hidden, w_down, preferred_element_type=jnp.float32)
    summed = lax.psum(partial_sum, "blk")
    after_mlp = (rows_full.astype(jnp.float32) + summed).astype(jnp.bfloat16)
    logits = jnp.dot(rms_round(after_mlp, head_gain), w_head, preferred_element_type=jnp.float32)
    request_count = logits.shape[0]
    half_rows = request_count // 2
    slot_scale = jnp.take(guide_scale, perm)
    request_order = (
        jnp.zeros((request_count,), jnp.int32)
        .at[perm]
        .set(jnp.arange(request_count, dtype=jnp.int32))
    )
    own_order = lax.dynamic_slice_in_dim(request_order, guide_index * half_rows, half_rows)
    other_logits = partner(logits.astype(jnp.bfloat16), "guide", 0).astype(logits.dtype)
    cond_logits = jnp.where(guide_index == 0, logits, other_logits)
    uncond_logits = jnp.where(guide_index == 0, other_logits, logits)
    mixed = (uncond_logits + slot_scale[:, None] * (cond_logits - uncond_logits)).astype(
        jnp.bfloat16
    )
    return jnp.take(mixed, own_order, axis=0)


def solution(mesh):
    def run(*args):
        chips = mesh.shape["blk"]
        rows, width = args[0].shape
        fits = chips == 16 and rows == 128 and mesh.shape["guide"] == 2 and width % (128 * chips) == 0
        return jax.shard_map(
            fast_body if fits else body,
            mesh=mesh,
            in_specs=(
                P(None, "blk"),
                P("blk", None),
                P("blk", None),
                P("guide", "blk", None, None),
                P("guide", None),
                P(),
                P(),
                P(),
                P(None, "blk"),
                P(),
                P(None, "blk"),
                P(None, "blk"),
                P("blk", None),
                P(),
                P(None, "blk"),
            ),
            out_specs=P("guide", "blk"),
            check_vma=False,
        )(*args)

    return run
```

```python
import functools

import jax
import jax.numpy as jnp
from jax import lax
from jax.experimental import pallas as pl
from jax.experimental.pallas import tpu as pltpu
from jax.sharding import PartitionSpec as P

FF = 10944
BF = jnp.bfloat16
F32 = jnp.float32
NN = (((1,), (0,)), ((), ()))
NT = (((1,), (1,)), ((), ()))
TN = (((0,), (0,)), ((), ()))
VM = pl.BlockSpec(memory_space=pltpu.VMEM)
HB = pl.BlockSpec(memory_space=pltpu.HBM)


def across(value, mask):
    chips = lax.axis_size("blk")
    pairs = [(d, (d ^ mask) ^ chips) for d in range(2 * chips)]
    return lax.ppermute(value, ("guide", "blk"), pairs)


def partner(value, axis, apart):
    mask = 2**apart
    pairs = [(source, source ^ mask) for source in range(lax.axis_size(axis))]
    return lax.ppermute(value, axis, pairs)


def swap(value, mask):
    pairs = [(source, source ^ mask) for source in range(lax.axis_size("blk"))]
    return lax.ppermute(value, "blk", pairs)


def rms_round(hidden, gain):
    values = hidden.astype(jnp.float32)
    meansq = jnp.mean(values * values, axis=-1, keepdims=True)
    return (values * lax.rsqrt(meansq + 1e-06) * gain).astype(jnp.bfloat16)


def cost(micros):
    return pl.CostEstimate(flops=int(micros * 1e9), bytes_accessed=int(micros * 3e6), transcendentals=0)


def iota(shape, dim):
    return lax.broadcasted_iota(jnp.int32, shape, dim)


def dot(a, b, dims, precision=None):
    return lax.dot_general(a, b, dims, precision=precision, preferred_element_type=F32)


def attend_kernel(
    perm_h, lengths_h, queries_h, new_h, cache, w_uv, out,
    perm, lengths, queries, new_kv, qs, keys, up, sems, others,
):
    slots, width, positions = cache.shape
    heads, latent, nope = w_uv.shape
    rows = heads * slots
    first = lax.axis_index("blk") * slots
    small = [
        pltpu.make_async_copy(source, target, others.at[k])
        for k, (source, target) in enumerate(
            ((queries_h, queries), (new_h, new_kv), (perm_h, perm), (lengths_h, lengths))
        )
    ]
    copies = [
        pltpu.make_async_copy(cache.at[s], keys.at[s], sems.at[s]) for s in range(slots)
    ]
    upcopy = pltpu.make_async_copy(w_uv, up, others.at[4])
    for copy in small + copies + [upcopy]:
        copy.start()
    small[0].wait()
    for h in range(heads):
        qs[h * slots : (h + 1) * slots, :] = queries[:, h * width : (h + 1) * width]
    q = qs[...]
    small[1].wait()
    new = new_kv[...]
    scale = (nope + width - latent) ** (-0.5)
    slot_of = iota((rows, 1), 0) % slots
    own = dot(q, new, NT)
    own = jnp.sum(jnp.where(iota((rows, slots), 1) == slot_of, own, 0.0), 1, keepdims=True) * scale
    small[2].wait()
    small[3].wait()
    live = jnp.zeros((rows, 1), jnp.int32)
    for s in range(slots):
        live = jnp.where(slot_of == s, lengths[0, perm[first + s]], live)
    for copy in copies:
        copy.wait()
    scores = jnp.zeros((rows, positions), F32)
    for s in range(slots):
        scores = jnp.where(slot_of == s, dot(q, keys[s], NN), scores)
    mask = iota((rows, positions), 1) < live
    scores = jnp.where(mask, scores * scale, -1e30)
    peak = jnp.maximum(jnp.max(scores, axis=1, keepdims=True), own)
    probs = jnp.where(mask, jnp.exp(scores - peak), 0.0)
    own = jnp.exp(own - peak)
    total = jnp.sum(probs, axis=1, keepdims=True) + own
    weights = probs / total
    own = (own / total).astype(BF).astype(F32)
    mixed = jnp.zeros((rows, latent), F32)
    for s in range(slots):
        part = jnp.where(slot_of == s, weights, 0.0).astype(BF)
        mixed += dot(part, keys[s, :latent, :], NT)
    mixed += own * jnp.tile(new[:, :latent].astype(F32), (heads, 1))
    upcopy.wait()
    for h in range(heads):
        rows_h = mixed[h * slots : (h + 1) * slots, :].astype(BF)
        out[:, h * nope : (h + 1) * nope] = dot(rows_h, up[h], NN).astype(BF)


def attend(perm, lengths, queries, new_kv, cache, w_uv):
    slots, width, positions = cache.shape
    heads, latent, nope = w_uv.shape
    return pl.pallas_call(
        attend_kernel,
        out_shape=jax.ShapeDtypeStruct((slots, heads * nope), BF),
        in_specs=[HB] * 6,
        out_specs=VM,
        scratch_shapes=[
            pltpu.SMEM(perm.shape, jnp.int32),
            pltpu.SMEM(lengths.shape, jnp.int32),
            pltpu.VMEM(queries.shape, BF),
            pltpu.VMEM(new_kv.shape, BF),
            pltpu.VMEM((heads * slots, width), BF),
            pltpu.VMEM((slots, width, positions), BF),
            pltpu.VMEM((heads, latent, nope), BF),
            pltpu.SemaphoreType.DMA((slots,)),
            pltpu.SemaphoreType.DMA((5,)),
        ],
        compiler_params=pltpu.CompilerParams(vmem_limit_bytes=60 << 20),
        cost_estimate=cost(15),
        name="attend",
    )(perm, lengths, queries, new_kv, cache, w_uv)


def project_kernel(perm, v3, v2, v1, v0, w_out, x_cols, out, full):
    blk = lax.axis_index("blk")
    rows = x_cols.shape[0]
    part = v0.shape[0]
    for q, ref in enumerate((v0, v1, v2, v3)):
        full[q * part : (q + 1) * part, :] = ref[...]
    attended = dot(full[...], w_out[...], NN)
    shape = (rows, rows)
    by_slot = (jnp.broadcast_to(perm[...], shape) == iota(shape, 0)).astype(F32)
    arrived = iota(shape, 1)
    slot = ((blk ^ (((arrived >> 3) & 3) * 4) ^ (arrived >> 5)) << 3) | (arrived & 7)
    move = (iota(shape, 0) == slot).astype(F32)
    by_arrival = dot(by_slot.astype(BF), move.astype(BF), NN)
    moved = dot(by_arrival, attended, NN, lax.Precision.HIGHEST)
    base = dot(by_slot.astype(BF), x_cols[...], NN)
    out[...] = (base + moved).astype(BF)


def project(perm, pieces, w_out, x_cols):
    return pl.pallas_call(
        project_kernel,
        out_shape=jax.ShapeDtypeStruct(x_cols.shape, BF),
        in_specs=[VM] * 7,
        out_specs=VM,
        scratch_shapes=[pltpu.VMEM((x_cols.shape[0], w_out.shape[0]), BF)],
        compiler_params=pltpu.CompilerParams(vmem_limit_bytes=4 << 20),
        cost_estimate=cost(15),
        name="project",
    )(perm, *reversed(pieces), w_out, x_cols)


def feed_kernel(
    r3, r2, r1, r0, gain, w_gate, w_up, w_down, own, c1, c2, c3, stay, go, full, acc
):
    blk = lax.axis_index("blk")
    groups, rows, cols = r0.shape
    units = w_gate.shape[0]
    for q, ref in enumerate((r0, r1, r2, r3)):
        for j in range(groups):
            at = pl.multiple_of((blk ^ (4 * j) ^ q) * cols, cols)
            full[:, pl.ds(at, cols)] = ref[j].astype(F32)
    values = full[...]
    meansq = jnp.mean(values * values, axis=1, keepdims=True)
    normed = (values * lax.rsqrt(meansq + 1e-06) * gain[...]).astype(BF)
    gate = dot(normed, w_gate[...], NT)
    up = dot(normed, w_up[...], NT)
    unit = blk * units + iota((rows, units), 1)
    hidden = gate * (1.0 / (1.0 + jnp.exp(-gate))) * up
    hidden = jnp.where(unit < FF, hidden, 0.0).astype(BF)
    acc[...] = dot(hidden, w_down[...], NN)
    low = blk & 3
    chunk = acc.shape[1] // 4
    for q, ref in enumerate((own, c1, c2, c3)):
        at = pl.multiple_of((low ^ q) * chunk, chunk)
        ref[...] = acc[:, pl.ds(at, chunk)].astype(ref.dtype)
    kept = full[:, pl.ds(pl.multiple_of(low * chunk, chunk), chunk)]
    first, last = kept[: rows // 2], kept[rows // 2 :]
    lower = lax.axis_index("guide") == 0
    stay[...] = jnp.where(lower, first, last).astype(BF)
    go[...] = jnp.where(lower, last, first).astype(BF)


def feed(pieces, gain, w_gate, w_up, w_down):
    groups, rows, cols = pieces[0].shape
    width = w_down.shape[1]
    part = (rows, width // 4)
    return pl.pallas_call(
        feed_kernel,
        out_shape=[
            jax.ShapeDtypeStruct(part, F32),
            jax.ShapeDtypeStruct(part, BF),
            jax.ShapeDtypeStruct(part, BF),
            jax.ShapeDtypeStruct(part, BF),
            jax.ShapeDtypeStruct((rows // 2, width // 4), BF),
            jax.ShapeDtypeStruct((rows // 2, width // 4), BF),
        ],
        in_specs=[VM] * 8,
        out_specs=[VM] * 6,
        scratch_shapes=[pltpu.VMEM((rows, width), F32), pltpu.VMEM((rows, width), F32)],
        compiler_params=pltpu.CompilerParams(vmem_limit_bytes=8 << 20),
        cost_estimate=cost(40),
        name="feed",
    )(*reversed(pieces), gain, w_gate, w_up, w_down)


def part_kernel(own, p1, p2, p3, stay, go):
    total = own[...] + p1[...].astype(F32) + p2[...].astype(F32) + p3[...].astype(F32)
    half = total.shape[0] // 2
    first, last = total[:half], total[half:]
    lower = lax.axis_index("guide") == 0
    stay[...] = jnp.where(lower, first, last).astype(BF)
    go[...] = jnp.where(lower, last, first).astype(BF)


def pair_kernel(a, b, c, d, out):
    half = a.shape[0]
    out[:half, :] = (a[...].astype(F32) + b[...].astype(F32)).astype(BF)
    out[half:, :] = (c[...].astype(F32) + d[...].astype(F32)).astype(BF)


def finish_kernel(own, other, stay, came, out):
    half = stay.shape[0]
    total = own[...].astype(F32) + other[...].astype(F32)
    for k, ref in enumerate((stay, came)):
        at = slice(k * half, (k + 1) * half)
        out[at, :] = (ref[...].astype(F32) + total[at]).astype(BF)


def small(kernel, name, shapes, *args):
    return pl.pallas_call(
        kernel,
        out_shape=[jax.ShapeDtypeStruct(shape, BF) for shape in shapes],
        in_specs=[VM] * len(args),
        out_specs=[VM] * len(shapes),
        compiler_params=pltpu.CompilerParams(vmem_limit_bytes=2 << 20),
        cost_estimate=cost(1),
        name=name,
    )(*args)


def block_product(ref, q, gain, w_head, at):
    width = ref.shape[1]
    first = pl.multiple_of(((lax.axis_index("blk") & 3) ^ q) * width, width)
    scaled = (ref[...].astype(F32) * gain[:, pl.ds(first, width)]).astype(BF)
    return dot(scaled, w_head[pl.ds(first, width), at], NN)


def open_kernel(piece, gain, w_head, acc, *, tile):
    @pl.loop(0, w_head.shape[1] // tile)
    def _(step):
        at = pl.ds(pl.multiple_of(step * tile, tile), tile)
        acc[:, at] = block_product(piece, 0, gain, w_head, at)


def more_kernel(piece, gain, w_head, old, acc, *, tile):
    @pl.loop(0, w_head.shape[1] // tile)
    def _(step):
        at = pl.ds(pl.multiple_of(step * tile, tile), tile)
        acc[:, at] = old[:, at] + block_product(piece, 3, gain, w_head, at)


def close_kernel(r0, r1, r2, r3, gain, scale, w_head, acc, out, factor, rms, done, sems):
    guide = lax.axis_index("guide")
    rows, width = r0.shape
    half = rows // 2
    tiles, _, tile = done.shape
    squares = jnp.zeros((rows, 1), F32)
    for ref in (r0, r1, r2, r3):
        values = ref[...].astype(F32)
        squares += jnp.sum(values * values, axis=1, keepdims=True)
    rms[...] = lax.rsqrt(squares / (4 * width) + 1e-06)
    mine = iota((half, rows), 0) + guide * half == iota((half, rows), 1)
    factor[...] = jnp.sum(
        jnp.where(mine, jnp.broadcast_to(scale[...], (half, rows)), 0.0), 1, keepdims=True
    )

    def store(step):
        at = pl.ds(pl.multiple_of(step * tile, tile), tile)
        return pltpu.make_async_copy(done.at[step], out.at[:, at], sems.at[step])

    @pl.loop(0, tiles)
    def _(step):
        at = pl.ds(pl.multiple_of(step * tile, tile), tile)
        logits = acc[:, at]
        for q, ref in ((2, r2), (1, r1)):
            logits += block_product(ref, q, gain, w_head, at)
        logits *= rms[...]
        own, other = logits[:half], logits[half:]
        cond = jnp.where(guide == 0, own, other)
        uncond = jnp.where(guide == 0, other, own)
        done[step] = (uncond + factor[...] * (cond - uncond)).astype(BF)
        store(step).start()

    @pl.loop(0, tiles)
    def _(step):
        store(step).wait()


def head(piece, scale, gain, w_head):
    rows, width = piece.shape
    vocab = w_head.shape[1]
    tile = next(t for t in (3200, 1280, 256, 128) if vocab % t == 0)
    pieces = [piece] + [swap(piece, mask) for mask in (1, 2, 3)]
    sums = jax.ShapeDtypeStruct((rows, vocab), F32)
    params = pltpu.CompilerParams(vmem_limit_bytes=4 << 20)
    acc = pl.pallas_call(
        functools.partial(open_kernel, tile=tile),
        out_shape=sums,
        in_specs=[VM] * 3,
        out_specs=VM,
        compiler_params=params,
        cost_estimate=cost(2),
        name="open",
    )(piece, gain, w_head)
    acc = pl.pallas_call(
        functools.partial(more_kernel, tile=tile),
        out_shape=sums,
        in_specs=[VM] * 4,
        out_specs=VM,
        input_output_aliases={3: 0},
        compiler_params=params,
        cost_estimate=cost(2),
        name="more",
    )(pieces[3], gain, w_head, acc)
    return pl.pallas_call(
        close_kernel,
        out_shape=jax.ShapeDtypeStruct((rows // 2, vocab), BF),
        in_specs=[VM] * 8,
        out_specs=HB,
        scratch_shapes=[
            pltpu.VMEM((rows // 2, 1), F32),
            pltpu.VMEM((rows, 1), F32),
            pltpu.VMEM((vocab // tile, rows // 2, tile), BF),
            pltpu.SemaphoreType.DMA((vocab // tile,)),
        ],
        compiler_params=pltpu.CompilerParams(vmem_limit_bytes=8 << 20),
        cost_estimate=cost(3),
        name="close",
    )(*pieces, gain, scale, w_head, acc)


def join_kernel(*refs):
    out = refs[-1]
    part = refs[0].shape[0]
    for k, ref in enumerate(refs[-2::-1]):
        out[k * part : (k + 1) * part, :] = ref[...]


def join(parts):
    rows, width = parts[0].shape
    return pl.pallas_call(
        join_kernel,
        out_shape=jax.ShapeDtypeStruct((len(parts) * rows, width), parts[0].dtype),
        in_specs=[VM] * len(parts),
        out_specs=VM,
        compiler_params=pltpu.CompilerParams(vmem_limit_bytes=1 << 20),
        cost_estimate=cost(1),
        name="join",
    )(*reversed(parts))


def spread(value, own):
    group = join([own] + [swap(value, mask) for mask in (4, 8, 12)])
    return [group] + [swap(group, mask) for mask in (1, 2, 3)]


def fast_body(
    x_cols,
    queries,
    new_kv,
    cache,
    lengths,
    perm,
    guide_scale,
    w_uv,
    w_out,
    mlp_gain,
    w_gate,
    w_up,
    w_down,
    head_gain,
    w_head,
):
    rows, cols = x_cols.shape
    keys = jnp.swapaxes(cache[0], 1, 2)
    values = attend(perm, lengths, queries, new_kv, keys, w_uv)
    residual = project(perm[None], spread(values, join([values])), w_out, x_cols)
    pieces = [piece.reshape(4, rows, cols) for piece in spread(residual, residual)]
    own, *chunks, stay, go = feed(
        pieces, mlp_gain[None], jnp.swapaxes(w_gate, 0, 1), jnp.swapaxes(w_up, 0, 1), w_down
    )
    came = partner(go, "guide", 0)
    arrived = [swap(chunk, mask) for chunk, mask in zip(chunks, (1, 2, 3))]
    came, arrived[0] = lax.optimization_barrier((came, arrived[0]))
    half, part = stay.shape, own.shape
    mine, his = small(part_kernel, "part", (half, half), own, *arrived)
    sums = (mine, swap(mine, 8), partner(his, "guide", 0), across(his, 8))
    (total,) = small(pair_kernel, "pair", (part,), *sums)
    (after,) = small(finish_kernel, "finish", (part,), total, swap(total, 4), stay, came)
    return head(after, guide_scale[None], head_gain[None], w_head)


def body(
    x_cols,
    queries,
    new_kv,
    cache,
    lengths,
    perm,
    guide_scale,
    w_uv,
    w_out,
    mlp_gain,
    w_gate,
    w_up,
    w_down,
    head_gain,
    w_head,
):
    guide_index = lax.axis_index("guide")
    blk_index = lax.axis_index("blk")
    slots_dev = queries.shape[0]
    heads_count = w_uv.shape[0]
    latent_size = w_uv.shape[1]
    key_width = new_kv.shape[1]
    score_scale = (w_uv.shape[2] + key_width - latent_size) ** (-0.5)
    slot_ids = blk_index * slots_dev + jnp.arange(slots_dev, dtype=jnp.int32)
    owners = jnp.take(perm, slot_ids)
    live_len = jnp.take(lengths[0], owners)
    query_heads = queries.reshape(slots_dev, heads_count, key_width)
    cached_keys = cache[0]
    scores = (
        jnp.einsum("shk,slk->shl", query_heads, cached_keys, preferred_element_type=jnp.float32)
        * score_scale
    )
    own_score = (
        jnp.einsum("shk,sk->sh", query_heads, new_kv, preferred_element_type=jnp.float32)
        * score_scale
    )
    live_mask = (
        jnp.arange(cached_keys.shape[1], dtype=jnp.int32)[None, None, :] < live_len[:, None, None]
    )
    scores = jnp.where(live_mask, scores, jnp.float32(-1e30))
    peak_score = jnp.maximum(jnp.max(scores, axis=-1), own_score)
    probs = jnp.where(live_mask, jnp.exp(scores - peak_score[..., None]), jnp.float32(0.0))
    own_prob = jnp.exp(own_score - peak_score)
    softmax_total = jnp.sum(probs, axis=-1) + own_prob
    weights = (probs / softmax_total[..., None]).astype(jnp.bfloat16)
    own_weight = (own_prob / softmax_total).astype(jnp.bfloat16)
    latent_out = jnp.einsum(
        "shl,slc->shc", weights, cached_keys[:, :, :latent_size], preferred_element_type=jnp.float32
    )
    latent_out = latent_out + own_weight.astype(jnp.float32)[..., None] * new_kv[
        :, None, :latent_size
    ].astype(jnp.float32)
    value_rows = jnp.einsum(
        "shc,hcd->shd", latent_out.astype(jnp.bfloat16), w_uv, preferred_element_type=jnp.float32
    )
    value_rows = value_rows.astype(jnp.bfloat16).reshape(slots_dev, -1)
    attended = jnp.dot(
        lax.all_gather(value_rows, "blk", axis=0, tiled=True),
        w_out,
        preferred_element_type=jnp.float32,
    )
    residual = (x_cols.astype(jnp.float32) + attended).astype(jnp.bfloat16)
    rows_full = lax.all_gather(residual, "blk", axis=1, tiled=True)
    normed = rms_round(rows_full, mlp_gain)
    unit_count = w_gate.shape[1]
    gate_out = jnp.dot(normed, w_gate, preferred_element_type=jnp.float32)
    up_out = jnp.dot(normed, w_up, preferred_element_type=jnp.float32)
    unit_ids = blk_index * unit_count + jnp.arange(unit_count, dtype=jnp.int32)
    hidden = jnp.where(
        unit_ids[None, :] < FF, jax.nn.silu(gate_out) * up_out, jnp.float32(0.0)
    ).astype(jnp.bfloat16)
    partial_sum = jnp.dot(hidden, w_down, preferred_element_type=jnp.float32)
    summed = lax.psum(partial_sum, "blk")
    after_mlp = (rows_full.astype(jnp.float32) + summed).astype(jnp.bfloat16)
    logits = jnp.dot(rms_round(after_mlp, head_gain), w_head, preferred_element_type=jnp.float32)
    request_count = logits.shape[0]
    half_rows = request_count // 2
    slot_scale = jnp.take(guide_scale, perm)
    request_order = (
        jnp.zeros((request_count,), jnp.int32)
        .at[perm]
        .set(jnp.arange(request_count, dtype=jnp.int32))
    )
    own_order = lax.dynamic_slice_in_dim(request_order, guide_index * half_rows, half_rows)
    other_logits = partner(logits.astype(jnp.bfloat16), "guide", 0).astype(logits.dtype)
    cond_logits = jnp.where(guide_index == 0, logits, other_logits)
    uncond_logits = jnp.where(guide_index == 0, other_logits, logits)
    mixed = (uncond_logits + slot_scale[:, None] * (cond_logits - uncond_logits)).astype(
        jnp.bfloat16
    )
    return jnp.take(mixed, own_order, axis=0)


def solution(mesh):
    def run(*args):
        chips = mesh.shape["blk"]
        rows, width = args[0].shape
        fits = chips == 16 and rows == 128 and mesh.shape["guide"] == 2 and width % (128 * chips) == 0
        return jax.shard_map(
            fast_body if fits else body,
            mesh=mesh,
            in_specs=(
                P(None, "blk"),
                P("blk", None),
                P("blk", None),
                P("guide", "blk", None, None),
                P("guide", None),
                P(),
                P(),
                P(),
                P(None, "blk"),
                P(),
                P(None, "blk"),
                P(None, "blk"),
                P("blk", None),
                P(),
                P(None, "blk"),
            ),
            out_specs=P("guide", "blk"),
            check_vma=False,
        )(*args)

    return run
```

```python
import functools

import jax
import jax.numpy as jnp
from jax import lax
from jax.experimental import pallas as pl
from jax.experimental.pallas import tpu as pltpu
from jax.sharding import PartitionSpec as P

FF = 10944
BF = jnp.bfloat16
F32 = jnp.float32
NN = (((1,), (0,)), ((), ()))
NT = (((1,), (1,)), ((), ()))
TN = (((0,), (0,)), ((), ()))
VM = pl.BlockSpec(memory_space=pltpu.VMEM)
HB = pl.BlockSpec(memory_space=pltpu.HBM)


def across(value, mask):
    chips = lax.axis_size("blk")
    pairs = [(d, (d ^ mask) ^ chips) for d in range(2 * chips)]
    return lax.ppermute(value, ("guide", "blk"), pairs)


def partner(value, axis, apart):
    mask = 2**apart
    pairs = [(source, source ^ mask) for source in range(lax.axis_size(axis))]
    return lax.ppermute(value, axis, pairs)


def swap(value, mask):
    pairs = [(source, source ^ mask) for source in range(lax.axis_size("blk"))]
    return lax.ppermute(value, "blk", pairs)


def rms_round(hidden, gain):
    values = hidden.astype(jnp.float32)
    meansq = jnp.mean(values * values, axis=-1, keepdims=True)
    return (values * lax.rsqrt(meansq + 1e-06) * gain).astype(jnp.bfloat16)


def cost(micros):
    return pl.CostEstimate(flops=int(micros * 1e9), bytes_accessed=int(micros * 3e6), transcendentals=0)


def iota(shape, dim):
    return lax.broadcasted_iota(jnp.int32, shape, dim)


def dot(a, b, dims, precision=None):
    return lax.dot_general(a, b, dims, precision=precision, preferred_element_type=F32)


def attend_kernel(
    perm_h, lengths_h, queries_h, new_h, cache, w_uv, out,
    perm, lengths, queries, new_kv, qs, keys, up, sems, others,
):
    slots, width, positions = cache.shape
    heads, latent, nope = w_uv.shape
    rows = heads * slots
    first = lax.axis_index("blk") * slots
    small = [
        pltpu.make_async_copy(source, target, others.at[k])
        for k, (source, target) in enumerate(
            ((queries_h, queries), (new_h, new_kv), (perm_h, perm), (lengths_h, lengths))
        )
    ]
    copies = [
        pltpu.make_async_copy(cache.at[s], keys.at[s], sems.at[s]) for s in range(slots)
    ]
    upcopy = pltpu.make_async_copy(w_uv, up, others.at[4])
    for copy in small + copies + [upcopy]:
        copy.start()
    small[0].wait()
    for h in range(heads):
        qs[h * slots : (h + 1) * slots, :] = queries[:, h * width : (h + 1) * width]
    q = qs[...]
    small[1].wait()
    new = new_kv[...]
    scale = (nope + width - latent) ** (-0.5)
    slot_of = iota((rows, 1), 0) % slots
    own = dot(q, new, NT)
    own = jnp.sum(jnp.where(iota((rows, slots), 1) == slot_of, own, 0.0), 1, keepdims=True) * scale
    small[2].wait()
    small[3].wait()
    live = jnp.zeros((rows, 1), jnp.int32)
    for s in range(slots):
        live = jnp.where(slot_of == s, lengths[0, perm[first + s]], live)
    for copy in copies:
        copy.wait()
    scores = jnp.zeros((rows, positions), F32)
    for s in range(slots):
        scores = jnp.where(slot_of == s, dot(q, keys[s], NN), scores)
    mask = iota((rows, positions), 1) < live
    scores = jnp.where(mask, scores * scale, -1e30)
    peak = jnp.maximum(jnp.max(scores, axis=1, keepdims=True), own)
    probs = jnp.where(mask, jnp.exp(scores - peak), 0.0)
    own = jnp.exp(own - peak)
    total = jnp.sum(probs, axis=1, keepdims=True) + own
    weights = probs / total
    own = (own / total).astype(BF).astype(F32)
    mixed = jnp.zeros((rows, latent), F32)
    for s in range(slots):
        part = jnp.where(slot_of == s, weights, 0.0).astype(BF)
        mixed += dot(part, keys[s, :latent, :], NT)
    mixed += own * jnp.tile(new[:, :latent].astype(F32), (heads, 1))
    upcopy.wait()
    for h in range(heads):
        rows_h = mixed[h * slots : (h + 1) * slots, :].astype(BF)
        out[:, h * nope : (h + 1) * nope] = dot(rows_h, up[h], NN).astype(BF)


def attend(perm, lengths, queries, new_kv, cache, w_uv):
    slots, width, positions = cache.shape
    heads, latent, nope = w_uv.shape
    return pl.pallas_call(
        attend_kernel,
        out_shape=jax.ShapeDtypeStruct((slots, heads * nope), BF),
        in_specs=[HB] * 6,
        out_specs=VM,
        scratch_shapes=[
            pltpu.SMEM(perm.shape, jnp.int32),
            pltpu.SMEM(lengths.shape, jnp.int32),
            pltpu.VMEM(queries.shape, BF),
            pltpu.VMEM(new_kv.shape, BF),
            pltpu.VMEM((heads * slots, width), BF),
            pltpu.VMEM((slots, width, positions), BF),
            pltpu.VMEM((heads, latent, nope), BF),
            pltpu.SemaphoreType.DMA((slots,)),
            pltpu.SemaphoreType.DMA((5,)),
        ],
        compiler_params=pltpu.CompilerParams(vmem_limit_bytes=60 << 20),
        cost_estimate=cost(15),
        name="attend",
    )(perm, lengths, queries, new_kv, cache, w_uv)


def project_kernel(perm, v3, v2, v1, v0, w_out, x_cols, out, full):
    blk = lax.axis_index("blk")
    rows = x_cols.shape[0]
    part = v0.shape[0]
    for q, ref in enumerate((v0, v1, v2, v3)):
        full[q * part : (q + 1) * part, :] = ref[...]
    attended = dot(full[...], w_out[...], NN)
    shape = (rows, rows)
    by_slot = (jnp.broadcast_to(perm[...], shape) == iota(shape, 0)).astype(F32)
    arrived = iota(shape, 1)
    slot = ((blk ^ (((arrived >> 3) & 3) * 4) ^ (arrived >> 5)) << 3) | (arrived & 7)
    move = (iota(shape, 0) == slot).astype(F32)
    by_arrival = dot(by_slot.astype(BF), move.astype(BF), NN)
    moved = dot(by_arrival, attended, NN, lax.Precision.HIGHEST)
    base = dot(by_slot.astype(BF), x_cols[...], NN)
    out[...] = (base + moved).astype(BF)


def project(perm, pieces, w_out, x_cols):
    return pl.pallas_call(
        project_kernel,
        out_shape=jax.ShapeDtypeStruct(x_cols.shape, BF),
        in_specs=[VM] * 7,
        out_specs=VM,
        scratch_shapes=[pltpu.VMEM((x_cols.shape[0], w_out.shape[0]), BF)],
        compiler_params=pltpu.CompilerParams(vmem_limit_bytes=4 << 20),
        cost_estimate=cost(15),
        name="project",
    )(perm, *reversed(pieces), w_out, x_cols)


def feed_kernel(
    r3, r2, r1, r0, gain, w_gate, w_up, w_down, own, c1, c2, c3, stay, go, full, acc
):
    blk = lax.axis_index("blk")
    groups, rows, cols = r0.shape
    units = w_gate.shape[0]
    for q, ref in enumerate((r0, r1, r2, r3)):
        for j in range(groups):
            at = pl.multiple_of((blk ^ (4 * j) ^ q) * cols, cols)
            full[:, pl.ds(at, cols)] = ref[j].astype(F32)
    values = full[...]
    meansq = jnp.mean(values * values, axis=1, keepdims=True)
    normed = (values * lax.rsqrt(meansq + 1e-06) * gain[...]).astype(BF)
    gate = dot(normed, w_gate[...], NT)
    up = dot(normed, w_up[...], NT)
    unit = blk * units + iota((rows, units), 1)
    hidden = gate * (1.0 / (1.0 + jnp.exp(-gate))) * up
    hidden = jnp.where(unit < FF, hidden, 0.0).astype(BF)
    acc[...] = dot(hidden, w_down[...], NN)
    low = blk & 3
    chunk = acc.shape[1] // 4
    for q, ref in enumerate((own, c1, c2, c3)):
        at = pl.multiple_of((low ^ q) * chunk, chunk)
        ref[...] = acc[:, pl.ds(at, chunk)].astype(ref.dtype)
    kept = full[:, pl.ds(pl.multiple_of(low * chunk, chunk), chunk)]
    first, last = kept[: rows // 2], kept[rows // 2 :]
    lower = lax.axis_index("guide") == 0
    stay[...] = jnp.where(lower, first, last).astype(BF)
    go[...] = jnp.where(lower, last, first).astype(BF)


def feed(pieces, gain, w_gate, w_up, w_down):
    groups, rows, cols = pieces[0].shape
    width = w_down.shape[1]
    part = (rows, width // 4)
    return pl.pallas_call(
        feed_kernel,
        out_shape=[
            jax.ShapeDtypeStruct(part, F32),
            jax.ShapeDtypeStruct(part, BF),
            jax.ShapeDtypeStruct(part, BF),
            jax.ShapeDtypeStruct(part, BF),
            jax.ShapeDtypeStruct((rows // 2, width // 4), BF),
            jax.ShapeDtypeStruct((rows // 2, width // 4), BF),
        ],
        in_specs=[VM] * 8,
        out_specs=[VM] * 6,
        scratch_shapes=[pltpu.VMEM((rows, width), F32), pltpu.VMEM((rows, width), F32)],
        compiler_params=pltpu.CompilerParams(vmem_limit_bytes=8 << 20),
        cost_estimate=cost(40),
        name="feed",
    )(*reversed(pieces), gain, w_gate, w_up, w_down)


def part_kernel(p3, p2, p1, own, stay, go):
    total = own[...] + p1[...].astype(F32) + p2[...].astype(F32) + p3[...].astype(F32)
    half = total.shape[0] // 2
    first, last = total[:half], total[half:]
    lower = lax.axis_index("guide") == 0
    stay[...] = jnp.where(lower, first, last).astype(BF)
    go[...] = jnp.where(lower, last, first).astype(BF)


def pair_kernel(d, c, b, a, out):
    half = a.shape[0]
    out[:half, :] = (a[...].astype(F32) + b[...].astype(F32)).astype(BF)
    out[half:, :] = (c[...].astype(F32) + d[...].astype(F32)).astype(BF)


def finish_kernel(own, other, stay, came, out):
    half = stay.shape[0]
    total = own[...].astype(F32) + other[...].astype(F32)
    for k, ref in enumerate((stay, came)):
        at = slice(k * half, (k + 1) * half)
        out[at, :] = (ref[...].astype(F32) + total[at]).astype(BF)


def small(kernel, name, shapes, *args):
    return pl.pallas_call(
        kernel,
        out_shape=[jax.ShapeDtypeStruct(shape, BF) for shape in shapes],
        in_specs=[VM] * len(args),
        out_specs=[VM] * len(shapes),
        compiler_params=pltpu.CompilerParams(vmem_limit_bytes=2 << 20),
        cost_estimate=cost(1),
        name=name,
    )(*args)


def block_product(ref, q, gain, w_head, at):
    width = ref.shape[1]
    first = pl.multiple_of(((lax.axis_index("blk") & 3) ^ q) * width, width)
    scaled = (ref[...].astype(F32) * gain[:, pl.ds(first, width)]).astype(BF)
    return dot(scaled, w_head[pl.ds(first, width), at], NN)


def open_kernel(piece, gain, w_head, acc, *, tile):
    @pl.loop(0, w_head.shape[1] // tile)
    def _(step):
        at = pl.ds(pl.multiple_of(step * tile, tile), tile)
        acc[:, at] = block_product(piece, 0, gain, w_head, at)


def more_kernel(piece, gain, w_head, old, acc, *, tile):
    @pl.loop(0, w_head.shape[1] // tile)
    def _(step):
        at = pl.ds(pl.multiple_of(step * tile, tile), tile)
        acc[:, at] = old[:, at] + block_product(piece, 3, gain, w_head, at)


def close_kernel(r0, r1, r2, r3, gain, scale, w_head, acc, out, factor, rms, done, sems):
    guide = lax.axis_index("guide")
    rows, width = r0.shape
    half = rows // 2
    tiles, _, tile = done.shape
    squares = jnp.zeros((rows, 1), F32)
    for ref in (r0, r1, r2, r3):
        values = ref[...].astype(F32)
        squares += jnp.sum(values * values, axis=1, keepdims=True)
    rms[...] = lax.rsqrt(squares / (4 * width) + 1e-06)
    mine = iota((half, rows), 0) + guide * half == iota((half, rows), 1)
    factor[...] = jnp.sum(
        jnp.where(mine, jnp.broadcast_to(scale[...], (half, rows)), 0.0), 1, keepdims=True
    )

    def store(step):
        at = pl.ds(pl.multiple_of(step * tile, tile), tile)
        return pltpu.make_async_copy(done.at[step], out.at[:, at], sems.at[step])

    @pl.loop(0, tiles)
    def _(step):
        at = pl.ds(pl.multiple_of(step * tile, tile), tile)
        logits = acc[:, at]
        for q, ref in ((2, r2), (1, r1)):
            logits += block_product(ref, q, gain, w_head, at)
        logits *= rms[...]
        own, other = logits[:half], logits[half:]
        cond = jnp.where(guide == 0, own, other)
        uncond = jnp.where(guide == 0, other, own)
        done[step] = (uncond + factor[...] * (cond - uncond)).astype(BF)
        store(step).start()

    @pl.loop(0, tiles)
    def _(step):
        store(step).wait()


def head(piece, scale, gain, w_head):
    rows, width = piece.shape
    vocab = w_head.shape[1]
    tile = next(t for t in (3200, 1280, 256, 128) if vocab % t == 0)
    pieces = [piece] + [swap(piece, mask) for mask in (1, 2, 3)]
    sums = jax.ShapeDtypeStruct((rows, vocab), F32)
    params = pltpu.CompilerParams(vmem_limit_bytes=4 << 20)
    acc = pl.pallas_call(
        functools.partial(open_kernel, tile=tile),
        out_shape=sums,
        in_specs=[VM] * 3,
        out_specs=VM,
        compiler_params=params,
        cost_estimate=cost(2),
        name="open",
    )(piece, gain, w_head)
    acc = pl.pallas_call(
        functools.partial(more_kernel, tile=tile),
        out_shape=sums,
        in_specs=[VM] * 4,
        out_specs=VM,
        input_output_aliases={3: 0},
        compiler_params=params,
        cost_estimate=cost(2),
        name="more",
    )(pieces[3], gain, w_head, acc)
    return pl.pallas_call(
        close_kernel,
        out_shape=jax.ShapeDtypeStruct((rows // 2, vocab), BF),
        in_specs=[VM] * 8,
        out_specs=HB,
        scratch_shapes=[
            pltpu.VMEM((rows // 2, 1), F32),
            pltpu.VMEM((rows, 1), F32),
            pltpu.VMEM((vocab // tile, rows // 2, tile), BF),
            pltpu.SemaphoreType.DMA((vocab // tile,)),
        ],
        compiler_params=pltpu.CompilerParams(vmem_limit_bytes=8 << 20),
        cost_estimate=cost(3),
        name="close",
    )(*pieces, gain, scale, w_head, acc)


def join_kernel(*refs):
    out = refs[-1]
    part = refs[0].shape[0]
    for k, ref in enumerate(refs[-2::-1]):
        out[k * part : (k + 1) * part, :] = ref[...]


def join(parts):
    rows, width = parts[0].shape
    return pl.pallas_call(
        join_kernel,
        out_shape=jax.ShapeDtypeStruct((len(parts) * rows, width), parts[0].dtype),
        in_specs=[VM] * len(parts),
        out_specs=VM,
        compiler_params=pltpu.CompilerParams(vmem_limit_bytes=1 << 20),
        cost_estimate=cost(1),
        name="join",
    )(*reversed(parts))


def spread(value, own):
    group = join([own] + [swap(value, mask) for mask in (4, 8, 12)])
    return [group] + [swap(group, mask) for mask in (1, 2, 3)]


def fast_body(
    x_cols,
    queries,
    new_kv,
    cache,
    lengths,
    perm,
    guide_scale,
    w_uv,
    w_out,
    mlp_gain,
    w_gate,
    w_up,
    w_down,
    head_gain,
    w_head,
):
    rows, cols = x_cols.shape
    keys = jnp.swapaxes(cache[0], 1, 2)
    values = attend(perm, lengths, queries, new_kv, keys, w_uv)
    residual = project(perm[None], spread(values, join([values])), w_out, x_cols)
    pieces = [piece.reshape(4, rows, cols) for piece in spread(residual, residual)]
    own, *chunks, stay, go = feed(
        pieces, mlp_gain[None], jnp.swapaxes(w_gate, 0, 1), jnp.swapaxes(w_up, 0, 1), w_down
    )
    came = partner(go, "guide", 0)
    arrived = [swap(chunk, mask) for chunk, mask in zip(chunks, (1, 2, 3))]
    came, arrived[0] = lax.optimization_barrier((came, arrived[0]))
    half, part = stay.shape, own.shape
    mine, his = small(part_kernel, "part", (half, half), *reversed(arrived), own)
    sums = (mine, swap(mine, 8), partner(his, "guide", 0), across(his, 8))
    (total,) = small(pair_kernel, "pair", (part,), *reversed(sums))
    (after,) = small(finish_kernel, "finish", (part,), total, swap(total, 4), stay, came)
    return head(after, guide_scale[None], head_gain[None], w_head)


def body(
    x_cols,
    queries,
    new_kv,
    cache,
    lengths,
    perm,
    guide_scale,
    w_uv,
    w_out,
    mlp_gain,
    w_gate,
    w_up,
    w_down,
    head_gain,
    w_head,
):
    guide_index = lax.axis_index("guide")
    blk_index = lax.axis_index("blk")
    slots_dev = queries.shape[0]
    heads_count = w_uv.shape[0]
    latent_size = w_uv.shape[1]
    key_width = new_kv.shape[1]
    score_scale = (w_uv.shape[2] + key_width - latent_size) ** (-0.5)
    slot_ids = blk_index * slots_dev + jnp.arange(slots_dev, dtype=jnp.int32)
    owners = jnp.take(perm, slot_ids)
    live_len = jnp.take(lengths[0], owners)
    query_heads = queries.reshape(slots_dev, heads_count, key_width)
    cached_keys = cache[0]
    scores = (
        jnp.einsum("shk,slk->shl", query_heads, cached_keys, preferred_element_type=jnp.float32)
        * score_scale
    )
    own_score = (
        jnp.einsum("shk,sk->sh", query_heads, new_kv, preferred_element_type=jnp.float32)
        * score_scale
    )
    live_mask = (
        jnp.arange(cached_keys.shape[1], dtype=jnp.int32)[None, None, :] < live_len[:, None, None]
    )
    scores = jnp.where(live_mask, scores, jnp.float32(-1e30))
    peak_score = jnp.maximum(jnp.max(scores, axis=-1), own_score)
    probs = jnp.where(live_mask, jnp.exp(scores - peak_score[..., None]), jnp.float32(0.0))
    own_prob = jnp.exp(own_score - peak_score)
    softmax_total = jnp.sum(probs, axis=-1) + own_prob
    weights = (probs / softmax_total[..., None]).astype(jnp.bfloat16)
    own_weight = (own_prob / softmax_total).astype(jnp.bfloat16)
    latent_out = jnp.einsum(
        "shl,slc->shc", weights, cached_keys[:, :, :latent_size], preferred_element_type=jnp.float32
    )
    latent_out = latent_out + own_weight.astype(jnp.float32)[..., None] * new_kv[
        :, None, :latent_size
    ].astype(jnp.float32)
    value_rows = jnp.einsum(
        "shc,hcd->shd", latent_out.astype(jnp.bfloat16), w_uv, preferred_element_type=jnp.float32
    )
    value_rows = value_rows.astype(jnp.bfloat16).reshape(slots_dev, -1)
    attended = jnp.dot(
        lax.all_gather(value_rows, "blk", axis=0, tiled=True),
        w_out,
        preferred_element_type=jnp.float32,
    )
    residual = (x_cols.astype(jnp.float32) + attended).astype(jnp.bfloat16)
    rows_full = lax.all_gather(residual, "blk", axis=1, tiled=True)
    normed = rms_round(rows_full, mlp_gain)
    unit_count = w_gate.shape[1]
    gate_out = jnp.dot(normed, w_gate, preferred_element_type=jnp.float32)
    up_out = jnp.dot(normed, w_up, preferred_element_type=jnp.float32)
    unit_ids = blk_index * unit_count + jnp.arange(unit_count, dtype=jnp.int32)
    hidden = jnp.where(
        unit_ids[None, :] < FF, jax.nn.silu(gate_out) * up_out, jnp.float32(0.0)
    ).astype(jnp.bfloat16)
    partial_sum = jnp.dot(hidden, w_down, preferred_element_type=jnp.float32)
    summed = lax.psum(partial_sum, "blk")
    after_mlp = (rows_full.astype(jnp.float32) + summed).astype(jnp.bfloat16)
    logits = jnp.dot(rms_round(after_mlp, head_gain), w_head, preferred_element_type=jnp.float32)
    request_count = logits.shape[0]
    half_rows = request_count // 2
    slot_scale = jnp.take(guide_scale, perm)
    request_order = (
        jnp.zeros((request_count,), jnp.int32)
        .at[perm]
        .set(jnp.arange(request_count, dtype=jnp.int32))
    )
    own_order = lax.dynamic_slice_in_dim(request_order, guide_index * half_rows, half_rows)
    other_logits = partner(logits.astype(jnp.bfloat16), "guide", 0).astype(logits.dtype)
    cond_logits = jnp.where(guide_index == 0, logits, other_logits)
    uncond_logits = jnp.where(guide_index == 0, other_logits, logits)
    mixed = (uncond_logits + slot_scale[:, None] * (cond_logits - uncond_logits)).astype(
        jnp.bfloat16
    )
    return jnp.take(mixed, own_order, axis=0)


def solution(mesh):
    def run(*args):
        chips = mesh.shape["blk"]
        rows, width = args[0].shape
        fits = chips == 16 and rows == 128 and mesh.shape["guide"] == 2 and width % (128 * chips) == 0
        return jax.shard_map(
            fast_body if fits else body,
            mesh=mesh,
            in_specs=(
                P(None, "blk"),
                P("blk", None),
                P("blk", None),
                P("guide", "blk", None, None),
                P("guide", None),
                P(),
                P(),
                P(),
                P(None, "blk"),
                P(),
                P(None, "blk"),
                P(None, "blk"),
                P("blk", None),
                P(),
                P(None, "blk"),
            ),
            out_specs=P("guide", "blk"),
            check_vma=False,
        )(*args)

    return run
```
